512 devices in a mesh: seq: 32 (over y, x, core), mp: 16 (over z).
Axes of the slice: x: 4, y: 4, z: 16, core: 2. Of those that a mesh axis runs over, the one named last changes fastest.
Arguments:
- enc_states: bfloat16 [98304, 1280], P(('seq', 'mp')), may hold values from -6 to 6
- dec_states: bfloat16 [98304, 1280], P(('seq', 'mp')), may hold values from -240 to 240
- segments: int32 [98304], P(('seq', 'mp')), may hold values from 0 to 30, as said below
- patch_keys: bfloat16 [15872, 1280], P(('seq', 'mp')), may hold values from -7 to 7
- w_in: bfloat16 [1280, 4096], P(None, 'mp'), may hold values from -0.15625 to 0.15625
- w_gate: bfloat16 [4096, 7168], P('seq', 'mp'), may hold values from -0.09375 to 0.09375
- w_up: bfloat16 [4096, 7168], P('seq', 'mp'), may hold values from -0.09375 to 0.09375
- w_down: bfloat16 [7168, 4096], P('mp', 'seq'), may hold values from -0.0625 to 0.0625
- w_out: bfloat16 [4096, 1280], P('mp'), may hold values from -0.09375 to 0.09375
Outputs:
- decoded: bfloat16 [98304, 1280], P(('seq', 'mp'))
The draws below stay inside these ranges and needn't reach their ends.
Inputs may be any that keep to these rules, and one draw needn't show every extreme that they name: `segments`: within each block of 192 bytes the patch number starts at 0 and rises by 0 or 1 from byte to byte. Block b belongs to device b, counted seq first; the blocks of the devices that share an mp index hold 512 patches together. A block holds at most 31 patches, and in every such set of blocks one holds exactly 31.
All inputs are finite; a program needn't handle non-finite values.
Results may differ from the reference program's by a relative error of at most 0.01.
Values may be sent and summed in bfloat16 or wider, within the bound.
A program may use at most 64 MiB of HBM per device.

```python
import math
import jax
import jax.numpy as jnp
from jax import lax

E = 1280
HD = 128
D = 4096
FFW = 7168
BYTE_DEV = 192
RMEAN = 16
PMAX = 31
BYTES = 98304
PATCHES = 15872
N_SEQ = 32
N_MP = 16


def counts_table(key):
    most_move = RMEAN // 3

    def column(column_key):
        shuffled = jax.random.permutation(jax.random.fold_in(column_key, 1), N_SEQ)
        shares = jax.random.randint(jax.random.fold_in(column_key, 2), (N_SEQ // 4,), 0, most_move + 1)
        shares = shares.at[0].set(most_move)
        ranking = jnp.zeros((N_SEQ,), jnp.int32).at[shuffled].set(jnp.arange(N_SEQ, dtype=jnp.int32))
        grouping = ranking // 4
        leader = ranking % 4 == 0
        amounts = shares[grouping]
        return jnp.where(leader, RMEAN + 3 * amounts, RMEAN - amounts).astype(jnp.int32)
    column_keys = jax.random.split(jax.random.fold_in(key, 11), N_MP)
    return jnp.transpose(jax.vmap(column)(column_keys))


def patch_numbers(key):
    totals = counts_table(key).reshape(N_SEQ * N_MP)

    def block(block_key, total):
        shuffled = jax.random.permutation(block_key, BYTE_DEV - 1)
        ranking = jnp.zeros((BYTE_DEV - 1,), jnp.int32).at[shuffled].set(jnp.arange(BYTE_DEV - 1, dtype=jnp.int32))
        is_cut = (ranking < total - 1).astype(jnp.int32)
        return jnp.concatenate([jnp.zeros((1,), jnp.int32), jnp.cumsum(is_cut).astype(jnp.int32)])
    block_keys = jax.random.split(jax.random.fold_in(key, 13), N_SEQ * N_MP)
    return jax.vmap(block)(block_keys, totals).reshape(BYTES)


def key_values(key):
    base = jnp.clip(jax.random.normal(jax.random.fold_in(key, 21), (PATCHES, E), jnp.float32), -6.0, 6.0)
    return base


def draw_segments(key, part):
    return patch_numbers(key)


def draw_patch_keys(key, part):
    return key_values(key).astype(jnp.bfloat16)


def draw_dec_states(key, part):
    base = jnp.clip(jax.random.normal(jax.random.fold_in(key, 31), (BYTES, E), jnp.float32), -6.0, 6.0)
    return base.astype(jnp.bfloat16)


def levels(key, dims, cuts, least, largest):
    def one(dim, blocks):
        draws = jax.random.uniform(jax.random.fold_in(jax.random.fold_in(key, 6), dim), (blocks,), jnp.float32, least / len(cuts), largest / len(cuts))
        return jnp.repeat(jnp.exp(draws), dims[dim] // blocks).reshape((-1,) + (1,) * (len(dims) - dim - 1))

    loudness = one(*cuts[0])
    for cut in cuts[1:]:
        loudness = loudness * one(*cut)
    return loudness


def bell_draw(rng, extent, spread, limit, pieces=(), kind=jnp.bfloat16):
    values = spread * jax.random.normal(rng, extent, jnp.float32)
    if pieces:
        values = values * levels(rng, extent, pieces, -0.22, 0.18)
    return jnp.clip(values, -limit, limit).astype(kind)


def setup_inputs(seed: int = 0) -> dict:
    key_of = jax.random.split(jax.random.key(seed), 10)
    enc_states = bell_draw(key_of[0], (BYTES, E), 1.0, 6.0, ((0, 512),))
    dec_states = draw_dec_states(jax.random.fold_in(key_of[9], 71), 0)
    segments = draw_segments(jax.random.fold_in(key_of[9], 71), 0)
    patch_keys = draw_patch_keys(jax.random.fold_in(key_of[9], 71), 0)
    w_in = bell_draw(key_of[4], (E, D), E ** -0.5, 0.15625, ((1, 16),))
    w_gate = bell_draw(key_of[5], (D, FFW), D ** -0.5, 0.09375, ((0, 32), (1, 16)))
    w_up = bell_draw(key_of[6], (D, FFW), D ** -0.5, 0.09375, ((0, 32), (1, 16)))
    w_down = bell_draw(key_of[7], (FFW, D), FFW ** -0.5, 0.0625, ((0, 16), (1, 32)))
    w_out = bell_draw(key_of[8], (D, E), D ** -0.5, 0.09375, ((0, 16),))
    return dict(enc_states=enc_states, dec_states=dec_states, segments=segments, patch_keys=patch_keys, w_in=w_in, w_gate=w_gate, w_up=w_up, w_down=w_down, w_out=w_out)


norm_epsilon = 1e-05

def reference(enc_states, dec_states, segments, patch_keys, w_in, w_gate, w_up, w_down, w_out):
    blocks = N_SEQ * N_MP
    heads = E // HD
    numbers = segments.reshape(blocks, BYTE_DEV)
    local_ids = jnp.arange(PMAX, dtype=jnp.int32)
    member = (numbers[:, None, :] == local_ids[None, :, None]).astype(jnp.float32)
    pool_sums = jnp.einsum('pjb,pbe->pje', member, enc_states.reshape(blocks, BYTE_DEV, E).astype(jnp.float32), precision=lax.Precision.HIGHEST)
    lengths = lax.optimization_barrier(jnp.sum(member, axis=2))
    pooled = (pool_sums / jnp.maximum(lengths, 1.0)[:, :, None]).astype(jnp.bfloat16)
    totals = numbers[:, BYTE_DEV - 1] + 1
    table = totals.reshape(N_SEQ, N_MP)
    starts = jnp.cumsum(table, axis=0).astype(jnp.int32) - table
    column_rows = N_SEQ * RMEAN
    all_rows = N_MP * column_rows
    first_row = (jnp.arange(N_MP, dtype=jnp.int32)[None, :] * column_rows + starts).reshape(blocks)
    index_rows = (first_row[:, None] + local_ids[None, :]).astype(jnp.int32)
    live = local_ids[None, :] < totals[:, None]
    target = jnp.where(live, index_rows, all_rows).astype(jnp.int32)
    packed = jnp.zeros((all_rows, E), jnp.bfloat16).at[target.reshape(-1)].set(pooled.reshape(blocks * PMAX, E), mode='drop')
    x_rows = jnp.dot(packed, w_in, preferred_element_type=jnp.float32).astype(jnp.bfloat16)
    x_wide = x_rows.astype(jnp.float32)
    square_mean = lax.optimization_barrier(jnp.mean(x_wide * x_wide, axis=1, keepdims=True))
    normed = (x_wide * lax.rsqrt(square_mean + norm_epsilon)).astype(jnp.bfloat16)
    gate = jnp.dot(normed, w_gate, preferred_element_type=jnp.float32)
    up = jnp.dot(normed, w_up, preferred_element_type=jnp.float32)
    hidden = (jax.nn.silu(gate) * up).astype(jnp.bfloat16)
    part_width = FFW // N_MP

    def add_part(total, index):
        piece_hidden = lax.dynamic_slice_in_dim(hidden, (index * part_width).astype(jnp.int32), part_width, 1)
        piece_weight = lax.dynamic_slice_in_dim(w_down, (index * part_width).astype(jnp.int32), part_width, 0)
        term = jnp.dot(piece_hidden, piece_weight, preferred_element_type=jnp.float32).astype(jnp.bfloat16)
        term = lax.optimization_barrier(term).astype(jnp.float32)
        return (total + term, None)
    down, _ = lax.scan(add_part, jnp.zeros((all_rows, D), jnp.float32), jnp.arange(N_MP, dtype=jnp.int32))
    residual = (x_wide + down).astype(jnp.bfloat16)
    model_part = D // N_MP

    def add_out(total, index):
        piece_rows = lax.dynamic_slice_in_dim(residual, (index * model_part).astype(jnp.int32), model_part, 1)
        piece_weight = lax.dynamic_slice_in_dim(w_out, (index * model_part).astype(jnp.int32), model_part, 0)
        term = jnp.dot(piece_rows, piece_weight, preferred_element_type=jnp.float32).astype(jnp.bfloat16)
        term = lax.optimization_barrier(term).astype(jnp.float32)
        return (total + term, None)
    out_sum, _ = lax.scan(add_out, jnp.zeros((all_rows, E), jnp.float32), jnp.arange(N_MP, dtype=jnp.int32))
    outputs = out_sum.astype(jnp.bfloat16)
    safe_rows = jnp.minimum(target, all_rows - 1).astype(jnp.int32)
    patch_values = jnp.take(outputs, safe_rows.reshape(-1), axis=0).reshape(blocks, PMAX, E)
    patch_values = jnp.where(live[:, :, None], patch_values, jnp.zeros_like(patch_values))
    queries = dec_states.reshape(blocks, BYTE_DEV, heads, HD).astype(jnp.float32)
    keys_local = patch_keys.reshape(blocks, PMAX, heads, HD).astype(jnp.float32)
    scores = jnp.einsum('pbhd,pjhd->phbj', queries, keys_local, precision=lax.Precision.HIGHEST) / math.sqrt(HD)
    allowed = local_ids[None, None, :] <= numbers[:, :, None]
    scores = jnp.where(allowed[:, None, :, :], scores, -1e+30)
    peak = lax.optimization_barrier(jnp.max(scores, axis=3, keepdims=True))
    expon = jnp.exp(scores - peak)
    weights = (expon / lax.optimization_barrier(jnp.sum(expon, axis=3, keepdims=True))).astype(jnp.bfloat16)
    values_local = patch_values.reshape(blocks, PMAX, heads, HD).astype(jnp.float32)
    mixed = jnp.einsum('phbj,pjhd->pbhd', weights.astype(jnp.float32), values_local, precision=lax.Precision.HIGHEST)
    return (dec_states.astype(jnp.float32) + mixed.reshape(BYTES, E)).astype(jnp.bfloat16)
```

```python
import functools
import math

import jax
import jax.numpy as jnp
from jax import lax
from jax.experimental import pallas as pl
from jax.experimental.pallas import tpu as pltpu
from jax.sharding import PartitionSpec as P

MESH = pl.DeviceIdType.MESH
HD = 128
SIDE = 4
NZ = 16
SLOTS = 32
BF = jnp.bfloat16
F32 = jnp.float32
EPS = 1e-05
NT = (((1,), (1,)), ((), ()))
UP_HOPS = 8
DOWN_HOPS = 7


def mm(a, b):
    return jnp.dot(a, b, preferred_element_type=F32)


def mm_nt(a, b):
    return lax.dot_general(a, b, NT, preferred_element_type=F32)


def kernel(
    enc_ref, dec_ref, seg_ref, keys_ref, win_ref, wg_ref, wu_ref, wd_ref, wout_ref,
    out_ref,
    rg, ru, rd, bc, ua, rsb, wf, pall, xo, st, ob, rzp, szp, rzm, szm, kpad, wts,
    raw_s, raw_r, loc_s, bc_r, bc_sp, bc_sm, rs_s, rs_r, w_s, w_r,
    p_r, p_sp, p_sm, st_r, st_sp, st_sm, zp_s, zp_r, zm_s, zm_r,
):
    s = lax.axis_index("seq")
    z = lax.axis_index("mp")
    k = s % 2
    x = (s // 2) % SIDE
    y = s // (2 * SIDE)
    a = x + k * (y - x)
    b = y + k * (x - y)
    width = enc_ref.shape[1]
    half = width // 2
    quarter = half // SIDE
    units = wg_ref.shape[1]
    pad = 512
    lanes = 3 * pad // SIDE
    depth = wg_ref.shape[0]

    def dev(xx, yy, kk, zz):
        return {"seq": (yy * SIDE + xx) * 2 + kk, "mp": zz}

    def x_peer(j, kk):
        return dev((x + j) % SIDE, y, kk, z)

    def y_peer(j, kk):
        return dev(x, (y + j) % SIDE, kk, z)

    def a_peer(j):
        return dev((x + j * (1 - k)) % SIDE, (y + j * k) % SIDE, k, z)

    def b_peer(j):
        return dev((x + j * k) % SIDE, (y + j * (1 - k)) % SIDE, k, z)

    partner = dev(x, y, 1 - k, z)
    above = dev(x, y, k, (z + 1) % NZ)
    below = dev(x, y, k, (z + NZ - 1) % NZ)

    barrier = pltpu.get_barrier_semaphore()
    greeted = [partner, above, below]
    for j in (1, 2, 3):
        for kk in (0, 1):
            greeted += [x_peer(j, kk), y_peer(j, kk)]
    for d in greeted:
        pl.semaphore_signal(barrier, inc=1, device_id=d, device_id_type=MESH)
    pl.semaphore_wait(barrier, len(greeted))

    def remote(src, dst, ssem, rsem, d):
        return pltpu.make_async_remote_copy(
            src_ref=src, dst_ref=dst, send_sem=ssem, recv_sem=rsem, device_id=d, device_id_type=MESH
        )

    raws = ((wg_ref, rg), (wu_ref, ru), (wd_ref, rd))
    raw_targets = [(partner, b)]
    raw_targets += [(x_peer(j, 0), x) for j in (1, 2, 3)]
    raw_targets += [(y_peer(j, 1), y) for j in (1, 2, 3)]
    raw_sends = []
    for n, (d, slot) in enumerate(raw_targets):
        for i, (src, dst) in enumerate(raws):
            c = remote(src, dst.at[slot, k], raw_s.at[n, i], raw_r.at[slot, k, i], d)
            c.start()
            raw_sends.append(c)
    raw_local = []
    for i, (src, dst) in enumerate(raws):
        c = pltpu.make_async_copy(src, dst.at[a, k], loc_s.at[i])
        c.start()
        raw_local.append(c)

    def source(zz):
        hit0 = (zz // SIDE) == y
        hit1 = (zz % SIDE) == x
        hit = jnp.where(k == 0, hit0, hit1)
        slot = jnp.where(k == 0, zz % SIDE, zz // SIDE)
        return hit, slot

    first_row = k * half + a * quarter

    def bc_send(slot, part, up):
        sems = bc_sp if up else bc_sm
        return remote(
            bc.at[slot, part], bc.at[slot, part], sems.at[slot, part], bc_r.at[slot, part],
            above if up else below,
        )

    hit_me, slot_me = source(z)

    @pl.when(hit_me)
    def _():
        bc[slot_me, 0] = win_ref[pl.ds(pl.multiple_of(first_row, 32), quarter), :]
        bc_send(slot_me, 0, True).start()
        bc_send(slot_me, 0, False).start()
        rows = lax.broadcasted_iota(jnp.int32, (quarter, width), 0) + first_row
        cols = lax.broadcasted_iota(jnp.int32, (quarter, width), 1)
        pick = jnp.where(rows == cols, 1.0, 0.0).astype(BF)
        bc[slot_me, 1] = mm_nt(pick, wout_ref[...]).astype(BF)
        bc_send(slot_me, 1, True).start()
        bc_send(slot_me, 1, False).start()

    def bc_step(t):
        hit_u, slot_u = source((z + NZ - t) % NZ)
        hit_d, slot_d = source((z + t) % NZ)
        for part in (0, 1):

            @pl.when(hit_u)
            def _():
                bc_send(slot_u, part, True).wait_recv()
                if t < UP_HOPS:
                    bc_send(slot_u, part, True).start()

            if t <= DOWN_HOPS:

                @pl.when(hit_d)
                def _():
                    bc_send(slot_d, part, False).wait_recv()
                    if t < DOWN_HOPS:
                        bc_send(slot_d, part, False).start()

    member = lax.broadcasted_iota(jnp.int32, (SLOTS, enc_ref.shape[0]), 0) == seg_ref[...]
    member = jnp.where(member, 1.0, 0.0)
    lengths = jnp.maximum(jnp.sum(member, axis=1, keepdims=True), 1.0)
    pall[z] = (mm(member.astype(BF), enc_ref[...]) / lengths).astype(BF)

    def ring_send(buf, slot, ssem, rsem, d):
        return remote(buf.at[slot], buf.at[slot], ssem.at[slot], rsem.at[slot], d)

    def ring_step(buf, sp, sm, r, t):
        if t == 0:
            ring_send(buf, z, sp, r, above).start()
            ring_send(buf, z, sm, r, below).start()
            return
        up_slot = (z + NZ - t) % NZ
        down_slot = (z + t) % NZ
        ring_send(buf, up_slot, sp, r, above).wait_recv()
        if t < UP_HOPS:
            ring_send(buf, up_slot, sp, r, above).start()
        if t <= DOWN_HOPS:
            ring_send(buf, down_slot, sm, r, below).wait_recv()
            if t < DOWN_HOPS:
                ring_send(buf, down_slot, sm, r, below).start()

    def ring_drain(buf, sp, sm, r):
        for t in range(UP_HOPS):
            ring_send(buf, (z + NZ - t) % NZ, sp, r, above).wait_send()
        for t in range(DOWN_HOPS):
            ring_send(buf, (z + t) % NZ, sm, r, below).wait_send()

    p_step = functools.partial(ring_step, pall, p_sp, p_sm, p_r)
    st_step = functools.partial(ring_step, st, st_sp, st_sm, st_r)

    ua[...] = jnp.zeros_like(ua)
    lag = 3
    for t in range(1, UP_HOPS + 1):
        bc_step(t)
        if t >= lag:
            p_step(t - lag)

    for c in raw_local:
        c.wait()
    for n, d in enumerate(range(SIDE)):
        for kk in (0, 1):
            for i, (src, dst) in enumerate(raws):

                @pl.when(jnp.logical_or(a != d, k != kk))
                def _():
                    remote(src, dst.at[d, kk], raw_s.at[0, 0], raw_r.at[d, kk, i], partner).wait_recv()

    acc_g = jnp.zeros((quarter, units), F32)
    acc_u = jnp.zeros((quarter, units), F32)
    acc_d = jnp.zeros((quarter, units), F32)
    for i in range(SIDE):
        for kk in (0, 1):
            ins = bc[i, 0][:, kk * depth : (kk + 1) * depth]
            outs = bc[i, 1][:, kk * depth : (kk + 1) * depth]
            acc_g += mm(ins, rg[i, kk])
            acc_u += mm(ins, ru[i, kk])
            acc_d += mm_nt(outs, rd[i, kk])
    ua[:, 0:units] = acc_g.astype(BF)
    ua[:, pad : pad + units] = acc_u.astype(BF)
    ua[:, 2 * pad : 2 * pad + units] = acc_d.astype(BF)

    def piece(bb):
        return pl.ds(pl.multiple_of(bb * lanes, 128), lanes)

    rs_copies = []
    for j in (1, 2, 3):
        c = remote(ua.at[:, piece((b + j) % SIDE)], rsb.at[j - 1], rs_s.at[j - 1], rs_r.at[j - 1], b_peer(j))
        c.start()
        rs_copies.append(c)

    p_step(UP_HOPS - lag + 1)

    def place(kk, aa, bb):
        row = pl.multiple_of(kk * half + aa * quarter, 32)
        return wf.at[pl.ds(row, quarter), piece(bb)]

    w_copies = []

    def w_send(kk, aa, bb, d):
        n = len(w_copies)
        c = remote(place(kk, aa, bb), place(kk, aa, bb), w_s.at[n], w_r.at[kk, aa, bb], d)
        c.start()
        w_copies.append(c)

    def w_wait(kk, aa, bb):
        remote(place(kk, aa, bb), place(kk, aa, bb), w_s.at[0], w_r.at[kk, aa, bb], partner).wait_recv()

    total = ua[:, piece(b)].astype(F32)
    for c in rs_copies:
        c.wait_recv()
    for j in (0, 1, 2):
        total += rsb[j].astype(F32)
    wf[pl.ds(pl.multiple_of(first_row, 32), quarter), piece(b)] = total.astype(BF)
    for j in (1, 2, 3):
        w_send(k, a, b, b_peer(j))
    for j in (1, 3, 2):
        w_send(k, a, b, a_peer(j))
    w_send(k, a, b, partner)

    p_step(UP_HOPS - lag + 2)
    for j in (1, 3, 2):
        bb = (b + j) % SIDE
        w_wait(k, a, bb)
        for i in (1, 3, 2):
            w_send(k, a, bb, a_peer(i))
        w_send(k, a, bb, partner)
    p_step(UP_HOPS)

    rows = NZ * SLOTS
    for lo in range(0, NZ, 4):
        pr = pall[lo : lo + 4].reshape(4 * SLOTS, width)
        xz = mm(pr, win_ref[...])
        xr = xz.astype(BF)
        sq = xr.astype(F32)
        sq = sq * sq
        sq = sq[:, 0:128] + sq[:, 128:256]
        share = jnp.sum(jnp.transpose(sq), axis=0, keepdims=True)
        st[z, :, lo * SLOTS : (lo + 4) * SLOTS] = jnp.broadcast_to(share, (8, 4 * SLOTS))
        ob[lo * SLOTS : (lo + 4) * SLOTS, :] = mm(xr, wout_ref[...])
    st_step(0)

    heads = width // HD
    kpad[...] = jnp.zeros_like(kpad)
    kpad[0 : keys_ref.shape[0], :] = keys_ref[...].astype(F32)
    own = lax.broadcasted_iota(jnp.int32, (heads * SLOTS, width), 0) // SLOTS
    own = own == lax.broadcasted_iota(jnp.int32, (heads * SLOTS, width), 1) // HD
    kb = jnp.where(own, jnp.concatenate([kpad[...]] * heads, axis=0), 0.0).astype(BF)
    scores = mm_nt(kb, dec_ref[...]) / math.sqrt(HD)
    allowed = lax.broadcasted_iota(jnp.int32, (SLOTS, dec_ref.shape[0]), 0) <= seg_ref[...]
    for h in range(heads):
        sc = jnp.where(allowed, scores[h * SLOTS : (h + 1) * SLOTS], -1e30)
        ex = jnp.exp(sc - jnp.max(sc, axis=0, keepdims=True))
        wts[h * SLOTS : (h + 1) * SLOTS, :] = ex / jnp.sum(ex, axis=0, keepdims=True)

    for t in range(1, UP_HOPS + 1):
        st_step(t)
    for j in (1, 3, 2):
        aa = (a + j) % SIDE
        for i in (0, 1, 3, 2):
            bb = (b + i) % SIDE
            w_wait(k, aa, bb)
            w_send(k, aa, bb, partner)
    for aa in range(SIDE):
        for bb in range(SIDE):
            w_wait(1 - k, aa, bb)

    stat = st[0, 0:1, :]
    for i in range(1, NZ):
        stat += st[i, 0:1, :]
    inv = lax.rsqrt(stat / (NZ * win_ref.shape[1]) + EPS)
    block = 128
    for lo in range(0, rows, block):
        pr = pall[lo // SLOTS : (lo + block) // SLOTS].reshape(block, width)
        r = jnp.transpose(jnp.broadcast_to(inv[:, lo : lo + block], (128, block)))
        r = jnp.concatenate([r] * (pad // 128), axis=1)
        g = mm(pr, wf[:, 0:pad]) * r
        u = mm(pr, wf[:, pad : 2 * pad]) * r
        hid = (g / (1.0 + jnp.exp(-g)) * u).astype(BF)
        ob[lo : lo + block, :] += mm_nt(hid, wf[:, 2 * pad : 3 * pad])

    cut = SLOTS // 2

    def part_of(dest, h):
        return ob[pl.ds(pl.multiple_of(dest * SLOTS + h * cut, cut), cut), :]

    zp_copies, zm_copies = {}, {}
    for t in range(UP_HOPS + 1):
        for h in (0, 1):
            if t < UP_HOPS:
                val = part_of((z + UP_HOPS - t) % NZ, h)
                if t:
                    zp_copies[t - 1, h].wait_recv()
                    val += rzp[t - 1, h].astype(F32)
                szp[t, h] = val.astype(BF)
                c = remote(szp.at[t, h], rzp.at[t, h], zp_s.at[t, h], zp_r.at[t, h], above)
                c.start()
                zp_copies[t, h] = c
            if t < DOWN_HOPS:
                val = part_of((z + NZ - DOWN_HOPS + t) % NZ, h)
                if t:
                    zm_copies[t - 1, h].wait_recv()
                    val += rzm[t - 1, h].astype(F32)
                szm[t, h] = val.astype(BF)
                c = remote(szm.at[t, h], rzm.at[t, h], zm_s.at[t, h], zm_r.at[t, h], below)
                c.start()
                zm_copies[t, h] = c

    wt = jnp.transpose(wts[...]).astype(BF)
    vals = []
    for h in (0, 1):
        zm_copies[DOWN_HOPS - 1, h].wait_recv()
        zp_copies[UP_HOPS - 1, h].wait_recv()
        val = part_of(z, h) + rzp[UP_HOPS - 1, h].astype(F32) + rzm[DOWN_HOPS - 1, h].astype(F32)
        vals.append(val)
    values = jnp.concatenate(vals, axis=0)
    vb = jnp.where(own, jnp.concatenate([values] * heads, axis=0), 0.0).astype(BF)
    out_ref[...] = (dec_ref[...].astype(F32) + mm(wt, vb)).astype(BF)

    for c in raw_sends + rs_copies + w_copies:
        c.wait_send()
    for i in range(SIDE):
        zi = jnp.where(k == 0, SIDE * y + i, SIDE * i + x)
        up_dist = (z - zi + NZ) % NZ
        down_dist = (zi - z + NZ) % NZ
        for part in (0, 1):

            @pl.when(up_dist < UP_HOPS)
            def _():
                bc_send(i, part, True).wait_send()

            @pl.when(down_dist < DOWN_HOPS)
            def _():
                bc_send(i, part, False).wait_send()

    ring_drain(pall, p_sp, p_sm, p_r)
    ring_drain(st, st_sp, st_sm, st_r)
    for c in (*zp_copies.values(), *zm_copies.values()):
        c.wait_send()


def body(enc_states, dec_states, segments, patch_keys, w_in, w_gate, w_up, w_down, w_out):
    nbytes, width = enc_states.shape
    depth, units = w_gate.shape
    quarter = width // 8
    rows = NZ * SLOTS
    dma = pltpu.SemaphoreType.DMA
    vmem = pltpu.VMEM
    return pl.pallas_call(
        kernel,
        out_shape=jax.ShapeDtypeStruct((nbytes, width), BF),
        in_specs=[pl.BlockSpec(memory_space=pltpu.VMEM)] * 9,
        out_specs=pl.BlockSpec(memory_space=pltpu.VMEM),
        scratch_shapes=[
            vmem((SIDE, 2, depth, units), BF),
            vmem((SIDE, 2, depth, units), BF),
            vmem((SIDE, 2, units, depth), BF),
            vmem((SIDE, 2, quarter, w_in.shape[1]), BF),
            vmem((quarter, 1536), BF),
            vmem((3, quarter, 384), BF),
            vmem((width, 1536), BF),
            vmem((NZ, SLOTS, width), BF),
            vmem((8, 128), F32),
            vmem((NZ, 8, rows), F32),
            vmem((rows, width), F32),
            vmem((UP_HOPS, 2, SLOTS // 2, width), BF),
            vmem((UP_HOPS, 2, SLOTS // 2, width), BF),
            vmem((DOWN_HOPS, 2, SLOTS // 2, width), BF),
            vmem((DOWN_HOPS, 2, SLOTS // 2, width), BF),
            vmem((SLOTS, width), F32),
            vmem((width // HD * SLOTS, nbytes), F32),
            dma((7, 3)), dma((SIDE, 2, 3)), dma((3,)),
            dma((SIDE, 2)), dma((SIDE, 2)), dma((SIDE, 2)),
            dma((3,)), dma((3,)), dma((40,)), dma((2, SIDE, SIDE)),
            dma((NZ,)), dma((NZ,)), dma((NZ,)),
            dma((NZ,)), dma((NZ,)), dma((NZ,)),
            dma((UP_HOPS, 2)), dma((UP_HOPS, 2)), dma((DOWN_HOPS, 2)), dma((DOWN_HOPS, 2)),
        ],
        compiler_params=pltpu.CompilerParams(
            collective_id=0, has_side_effects=True, vmem_limit_bytes=60 * 1024 * 1024
        ),
    )(enc_states, dec_states, segments.reshape(1, nbytes), patch_keys, w_in, w_gate, w_up, w_down, w_out)


def solution(mesh):
    placed = (
        P(("seq", "mp"), None),
        P(("seq", "mp"), None),
        P(("seq", "mp")),
        P(("seq", "mp"), None),
        P(None, "mp"),
        P("seq", "mp"),
        P("seq", "mp"),
        P("mp", "seq"),
        P("mp", None),
    )
    return jax.shard_map(
        body, mesh=mesh, in_specs=placed, out_specs=P(("seq", "mp"), None), check_vma=False
    )
```

```python
import math

import jax
import jax.numpy as jnp
from jax import lax
from jax.experimental import pallas as pl
from jax.experimental.pallas import tpu as pltpu
from jax.sharding import PartitionSpec as P

MESH = pl.DeviceIdType.MESH
HD = 128
SIDE = 4
NZ = 16
SLOTS = 32
CUT = SLOTS // 2
BF = jnp.bfloat16
F32 = jnp.float32
EPS = 1e-05
NT = (((1,), (1,)), ((), ()))
UP_HOPS = 8
DOWN_HOPS = 7
PAD = 512
LANES = (2 * PAD // SIDE, PAD // SIDE)


def mm(a, b):
    return jnp.dot(a, b, preferred_element_type=F32)


def mm_nt(a, b):
    return lax.dot_general(a, b, NT, preferred_element_type=F32)


def kernel(
    enc_hbm, dec_hbm, seg_ref, keys_ref, win_hbm, wg_hbm, wu_hbm, wd_hbm, wout_hbm,
    out_ref,
    enc_ref, dec_ref, win_ref, wout_ref,
    rg, ru, rd, bc, ug, ud, rsg, rsd, wf, pall, st, rc, ob, rzp, szp, rzm, szm, kpad, wts,
    in_s, raw_s, raw_r, loc_s, src_s, bc_r, bc_sp, bc_sm, rs_s, rs_r, w_s, w_r,
    p_r, p_sp, p_sm, st_r, st_s, zp_s, zp_r, zm_s, zm_r,
):
    s = lax.axis_index("seq")
    z = lax.axis_index("mp")
    k = s % 2
    x = (s // 2) % SIDE
    y = s // (2 * SIDE)
    a = x + k * (y - x)
    b = y + k * (x - y)
    width = enc_ref.shape[1]
    half = width // 2
    quarter = half // SIDE
    eighth = quarter // 2
    units = wg_hbm.shape[0]

    def dev(xx, yy, kk, zz):
        return {"seq": (yy * SIDE + xx) * 2 + kk, "mp": zz}

    def x_peer(j, kk):
        return dev((x + j) % SIDE, y, kk, z)

    def y_peer(j, kk):
        return dev(x, (y + j) % SIDE, kk, z)

    def a_peer(j):
        return dev((x + j * (1 - k)) % SIDE, (y + j * k) % SIDE, k, z)

    def b_peer(j):
        return dev((x + j * k) % SIDE, (y + j * (1 - k)) % SIDE, k, z)

    def z_peer(j):
        return dev(x, y, k, (z + j) % NZ)

    partner = dev(x, y, 1 - k, z)
    above = z_peer(1)
    below = z_peer(NZ - 1)

    barrier = pltpu.get_barrier_semaphore()
    greeted = [above, below, partner]
    for j in (2, 1, 3):
        for kk in (0, 1):
            greeted += [x_peer(j, kk), y_peer(j, kk)]
    for d in greeted:
        pl.semaphore_signal(barrier, inc=1, device_id=d, device_id_type=MESH)

    def remote(src, dst, ssem, rsem, d):
        return pltpu.make_async_remote_copy(
            src_ref=src, dst_ref=dst, send_sem=ssem, recv_sem=rsem, device_id=d, device_id_type=MESH
        )

    loads = []
    for i, (src, dst) in enumerate(
        ((wout_hbm, wout_ref), (enc_hbm, enc_ref), (win_hbm, win_ref), (dec_hbm, dec_ref))
    ):
        c = pltpu.make_async_copy(src, dst, in_s.at[i])
        c.start()
        loads.append(c)

    def source(zz):
        hit0 = (zz // SIDE) == y
        hit1 = (zz % SIDE) == x
        hit = jnp.where(k == 0, hit0, hit1)
        slot = jnp.where(k == 0, zz % SIDE, zz // SIDE)
        return hit, slot

    first_row = k * half + a * quarter
    hit_me, slot_me = source(z)

    def src_copy(h):
        row = pl.multiple_of(first_row + h * eighth, 16)
        return pltpu.make_async_copy(win_hbm.at[pl.ds(row, eighth), :], bc.at[slot_me, h], src_s.at[h])

    @pl.when(hit_me)
    def _():
        src_copy(0).start()
        src_copy(1).start()

    raws = ((wg_hbm, rg), (wu_hbm, ru), (wd_hbm, rd))
    raw_local = []
    for i, (src, dst) in enumerate(raws):
        c = pltpu.make_async_copy(src, dst.at[a, k], loc_s.at[i])
        c.start()
        raw_local.append(c)

    pl.semaphore_wait(barrier, len(greeted))

    def bc_send(slot, part, up):
        sems = bc_sp if up else bc_sm
        return remote(
            bc.at[slot, part], bc.at[slot, part], sems.at[slot, part], bc_r.at[slot, part],
            above if up else below,
        )

    @pl.when(hit_me)
    def _():
        for h in (0, 1):
            src_copy(h).wait()
            bc_send(slot_me, h, True).start()
            bc_send(slot_me, h, False).start()

    raw_targets = [(partner, b)]
    for j in (1, 3, 2):
        raw_targets += [(x_peer(j, 0), x), (y_peer(j, 1), y)]
    raw_sends = []
    for i, (src, dst) in enumerate(raws):
        for n, (d, slot) in enumerate(raw_targets):
            c = remote(src, dst.at[slot, k], raw_s.at[n, i], raw_r.at[slot, k, i], d)
            c.start()
            raw_sends.append(c)

    loads[0].wait()

    @pl.when(hit_me)
    def _():
        rows = lax.broadcasted_iota(jnp.int32, (quarter, width), 0) + first_row
        cols = lax.broadcasted_iota(jnp.int32, (quarter, width), 1)
        pick = jnp.where(rows == cols, 1.0, 0.0).astype(BF)
        turned = mm_nt(pick, wout_ref[...]).astype(BF)
        for h in (0, 1):
            bc[slot_me, 2 + h] = turned[h * eighth : (h + 1) * eighth]
            bc_send(slot_me, 2 + h, True).start()
            bc_send(slot_me, 2 + h, False).start()

    def bc_step(t, parts):
        if not 1 <= t <= UP_HOPS:
            return
        hit_u, slot_u = source((z + NZ - t) % NZ)
        hit_d, slot_d = source((z + t) % NZ)
        for part in parts:

            @pl.when(hit_u)
            def _():
                bc_send(slot_u, part, True).wait_recv()
                if t < UP_HOPS:
                    bc_send(slot_u, part, True).start()

            if t <= DOWN_HOPS:

                @pl.when(hit_d)
                def _():
                    bc_send(slot_d, part, False).wait_recv()
                    if t < DOWN_HOPS:
                        bc_send(slot_d, part, False).start()

    loads[1].wait()
    member = lax.broadcasted_iota(jnp.int32, (SLOTS, enc_ref.shape[0]), 0) == seg_ref[...]
    member = jnp.where(member, 1.0, 0.0)
    lengths = jnp.maximum(jnp.sum(member, axis=1, keepdims=True), 1.0)
    pall[z] = (mm(member.astype(BF), enc_ref[...]) / lengths).astype(BF)

    def p_send(slot, h, up):
        view = pall.at[slot, pl.ds(h * CUT, CUT), :]
        ssem = p_sp if up else p_sm
        return remote(view, view, ssem.at[slot, h], p_r.at[slot, h], above if up else below)

    def p_step(t):
        if not 0 <= t <= UP_HOPS:
            return
        up_slot = (z + NZ - t) % NZ
        down_slot = (z + t) % NZ
        for h in (0, 1):
            if t:
                p_send(up_slot, h, True).wait_recv()
            if t < UP_HOPS:
                p_send(up_slot, h, True).start()
            if 1 <= t <= DOWN_HOPS:
                p_send(down_slot, h, False).wait_recv()
            if t < DOWN_HOPS:
                p_send(down_slot, h, False).start()

    ug[...] = jnp.zeros_like(ug)
    ud[...] = jnp.zeros_like(ud)
    lag = 2
    for t in range(1, UP_HOPS + 1):
        bc_step(t, (0, 1))
        bc_step(t - 1, (2, 3))
        p_step(t - lag)

    def raw_wait(i):
        raw_local[i].wait()
        src, dst = raws[i]
        for d in range(SIDE):
            for kk in (0, 1):

                @pl.when(jnp.logical_or(a != d, k != kk))
                def _():
                    remote(src, dst.at[d, kk], raw_s.at[0, 0], raw_r.at[d, kk, i], partner).wait_recv()

    def deep(buf):
        return jnp.concatenate([buf[i, kk] for i in range(SIDE) for kk in (0, 1)], axis=1)

    def tall(part):
        return jnp.concatenate(
            [jnp.concatenate([bc[i, part + h] for i in range(SIDE)], axis=1) for h in (0, 1)], axis=0
        )

    rs_copies = [[], []]

    def piece(part, bb, base=0):
        return pl.ds(pl.multiple_of(base + bb * LANES[part], 128), LANES[part])

    def rs_send(part):
        src, dst = ((ug, rsg), (ud, rsd))[part]
        for j in (2, 1, 3):
            c = remote(
                src.at[:, piece(part, (b + j) % SIDE)], dst.at[j - 1],
                rs_s.at[part, j - 1], rs_r.at[part, j - 1], b_peer(j),
            )
            c.start()
            rs_copies[part].append(c)

    raw_wait(0)
    raw_wait(1)
    ins = tall(0)
    ug[:, 0:units] = mm_nt(ins, deep(rg)).astype(BF)
    ug[:, PAD : PAD + units] = mm_nt(ins, deep(ru)).astype(BF)
    rs_send(0)
    bc_step(UP_HOPS, (2, 3))
    p_step(UP_HOPS - lag + 1)
    raw_wait(2)
    outs = tall(2)
    down = jnp.zeros((quarter, units), F32)
    for i in range(SIDE):
        for kk in (0, 1):
            down += mm_nt(
                outs[:, (2 * i + kk) * HD : (2 * i + kk + 1) * HD], rd[i, kk]
            )
    ud[:, 0:units] = down.astype(BF)
    rs_send(1)

    def place(part, kk, aa, bb):
        row = pl.multiple_of(kk * half + aa * quarter, 32)
        return wf.at[pl.ds(row, quarter), piece(part, bb, part * 2 * PAD)]

    w_copies = []

    def w_send(part, kk, aa, bb, d):
        n = len(w_copies)
        view = place(part, kk, aa, bb)
        c = remote(view, view, w_s.at[n], w_r.at[part, kk, aa, bb], d)
        c.start()
        w_copies.append(c)

    def w_wait(part, kk, aa, bb):
        view = place(part, kk, aa, bb)
        remote(view, view, w_s.at[0], w_r.at[part, kk, aa, bb], partner).wait_recv()

    def w_sum(part):
        src, got = ((ug, rsg), (ud, rsd))[part]
        total = src[:, piece(part, b)].astype(F32)
        for c in rs_copies[part]:
            c.wait_recv()
        for j in (0, 1, 2):
            total += got[j].astype(F32)
        place(part, k, a, b)[...] = total.astype(BF)
        for j in (2, 1, 3):
            w_send(part, k, a, b, b_peer(j))
        for j in (2, 1, 3):
            w_send(part, k, a, b, a_peer(j))
        w_send(part, k, a, b, partner)

    def w_pass(part):
        for j in (1, 3, 2):
            bb = (b + j) % SIDE
            w_wait(part, k, a, bb)
            for i in (2, 1, 3):
                w_send(part, k, a, bb, a_peer(i))
            w_send(part, k, a, bb, partner)

    w_sum(0)
    p_step(UP_HOPS - lag + 2)
    w_sum(1)
    w_pass(0)

    loads[2].wait()
    rows = NZ * SLOTS
    for lo in range(0, NZ, 4):
        pr = pall[lo : lo + 4].reshape(4 * SLOTS, width)
        xr = mm(pr, win_ref[...]).astype(BF)
        sq = xr.astype(F32)
        sq = sq * sq
        sq = sq[:, 0:128] + sq[:, 128:256]
        st[z, :, lo * SLOTS : (lo + 4) * SLOTS] = jnp.sum(jnp.transpose(sq), axis=0, keepdims=True)
        ob[lo * SLOTS : (lo + 4) * SLOTS, :] = mm(xr, wout_ref[...])
    st_copies = []
    for j in (8, 7, 9, 6, 10, 5, 11, 4, 12, 3, 13, 2, 14, 1, 15):
        c = remote(st.at[z], st.at[z], st_s.at[j], st_r.at[z], z_peer(j))
        c.start()
        st_copies.append(c)
    w_pass(1)

    loads[3].wait()
    heads = width // HD
    kpad[...] = jnp.zeros_like(kpad)
    kpad[0 : keys_ref.shape[0], :] = keys_ref[...].astype(F32)
    own = lax.broadcasted_iota(jnp.int32, (heads * SLOTS, width), 0) // SLOTS
    own = own == lax.broadcasted_iota(jnp.int32, (heads * SLOTS, width), 1) // HD
    kb = jnp.where(own, jnp.concatenate([kpad[...]] * heads, axis=0), 0.0).astype(BF)
    scores = mm_nt(kb, dec_ref[...]) / math.sqrt(HD)
    allowed = lax.broadcasted_iota(jnp.int32, (SLOTS, dec_ref.shape[0]), 0) <= seg_ref[...]
    for h in range(heads):
        sc = jnp.where(allowed, scores[h * SLOTS : (h + 1) * SLOTS], -1e30)
        ex = jnp.exp(sc - jnp.max(sc, axis=0, keepdims=True))
        wts[h * SLOTS : (h + 1) * SLOTS, :] = ex / jnp.sum(ex, axis=0, keepdims=True)
    wt = jnp.transpose(wts[...]).astype(BF)

    for part in (0, 1):
        for j in (1, 3, 2):
            aa = (a + j) % SIDE
            for i in (0, 1, 3, 2):
                bb = (b + i) % SIDE
                w_wait(part, k, aa, bb)
                w_send(part, k, aa, bb, partner)

    for j in range(1, NZ):
        slot = (z + j) % NZ
        remote(st.at[slot], st.at[slot], st_s.at[0], st_r.at[slot], above).wait_recv()
    stat = st[0]
    for i in range(1, NZ):
        stat += st[i]
    inv = lax.rsqrt(stat / (NZ * win_ref.shape[1]) + EPS)
    for i in range(0, NZ, 4):
        r = jnp.transpose(jnp.broadcast_to(inv[:, i * SLOTS : (i + 4) * SLOTS], (HD, 4 * SLOTS)))
        rc[i : i + 4] = r.reshape(4, SLOTS, HD)

    for part in (0, 1):
        for aa in range(SIDE):
            for bb in range(SIDE):
                w_wait(part, 1 - k, aa, bb)

    def ffn(t):
        d1 = (z + UP_HOPS - t) % NZ
        d2 = (z + NZ - DOWN_HOPS + t) % NZ
        pr = jnp.concatenate([pall[d1], pall[d2]], axis=0)
        r = jnp.concatenate([rc[d1], rc[d2]], axis=0)
        r = jnp.concatenate([r] * (PAD // HD), axis=1)
        g = mm(pr, wf[:, 0:PAD]) * r
        u = mm(pr, wf[:, PAD : 2 * PAD]) * r
        hid = (g / (1.0 + jnp.exp(-g)) * u).astype(BF)
        o = mm_nt(hid, wf[:, 2 * PAD : 3 * PAD])
        row1 = pl.multiple_of(d1 * SLOTS, SLOTS)
        row2 = pl.multiple_of(d2 * SLOTS, SLOTS)
        return (
            o[0:SLOTS] + ob[pl.ds(row1, SLOTS), :],
            o[SLOTS : 2 * SLOTS] + ob[pl.ds(row2, SLOTS), :],
        )

    zp_copies, zm_copies = {}, {}
    for t in range(UP_HOPS):
        up_val, down_val = ffn(t)
        for h in (0, 1):
            val = up_val[h * CUT : (h + 1) * CUT]
            if t:
                zp_copies[t - 1, h].wait_recv()
                val += rzp[t - 1, h].astype(F32)
            szp[t, h] = val.astype(BF)
            c = remote(szp.at[t, h], rzp.at[t, h], zp_s.at[t, h], zp_r.at[t, h], above)
            c.start()
            zp_copies[t, h] = c
            if t < DOWN_HOPS:
                val = down_val[h * CUT : (h + 1) * CUT]
                if t:
                    zm_copies[t - 1, h].wait_recv()
                    val += rzm[t - 1, h].astype(F32)
                szm[t, h] = val.astype(BF)
                c = remote(szm.at[t, h], rzm.at[t, h], zm_s.at[t, h], zm_r.at[t, h], below)
                c.start()
                zm_copies[t, h] = c

    vals = []
    for h in (0, 1):
        zm_copies[DOWN_HOPS - 1, h].wait_recv()
        val = down_val[h * CUT : (h + 1) * CUT] + rzm[DOWN_HOPS - 1, h].astype(F32)
        zp_copies[UP_HOPS - 1, h].wait_recv()
        vals.append(val + rzp[UP_HOPS - 1, h].astype(F32))
    values = jnp.concatenate(vals, axis=0)
    vb = jnp.where(own, jnp.concatenate([values] * heads, axis=0), 0.0).astype(BF)
    out_ref[...] = mm(wt, vb)

    for c in raw_sends + rs_copies[0] + rs_copies[1] + w_copies + st_copies:
        c.wait_send()
    for i in range(SIDE):
        zi = jnp.where(k == 0, SIDE * y + i, SIDE * i + x)
        up_dist = (z - zi + NZ) % NZ
        down_dist = (zi - z + NZ) % NZ
        for part in range(4):

            @pl.when(up_dist < UP_HOPS)
            def _():
                bc_send(i, part, True).wait_send()

            @pl.when(down_dist < DOWN_HOPS)
            def _():
                bc_send(i, part, False).wait_send()

    for h in (0, 1):
        for t in range(UP_HOPS):
            p_send((z + NZ - t) % NZ, h, True).wait_send()
        for t in range(DOWN_HOPS):
            p_send((z + t) % NZ, h, False).wait_send()
    for c in (*zp_copies.values(), *zm_copies.values()):
        c.wait_send()


def body(enc_states, dec_states, segments, patch_keys, w_in, w_gate, w_up, w_down, w_out):
    nbytes, width = enc_states.shape
    depth, units = w_gate.shape
    local = w_in.shape[1]
    quarter = width // 8
    rows = NZ * SLOTS
    dma = pltpu.SemaphoreType.DMA
    vmem = pltpu.VMEM
    hbm = pl.BlockSpec(memory_space=pl.ANY)
    here = pl.BlockSpec(memory_space=pltpu.VMEM)
    mixed = pl.pallas_call(
        kernel,
        out_shape=jax.ShapeDtypeStruct((nbytes, width), F32),
        in_specs=[hbm, hbm, here, here, hbm, hbm, hbm, hbm, hbm],
        out_specs=here,
        scratch_shapes=[
            vmem((nbytes, width), BF),
            vmem((nbytes, width), BF),
            vmem((width, local), BF),
            vmem((local, width), BF),
            vmem((SIDE, 2, units, depth), BF),
            vmem((SIDE, 2, units, depth), BF),
            vmem((SIDE, 2, units, depth), BF),
            vmem((SIDE, 4, quarter // 2, local), BF),
            vmem((quarter, 2 * PAD), BF),
            vmem((quarter, PAD), BF),
            vmem((3, quarter, LANES[0]), BF),
            vmem((3, quarter, LANES[1]), BF),
            vmem((width, 3 * PAD), BF),
            vmem((NZ, SLOTS, width), BF),
            vmem((NZ, 1, rows), F32),
            vmem((NZ, SLOTS, HD), F32),
            vmem((rows, width), F32),
            vmem((UP_HOPS, 2, CUT, width), BF),
            vmem((UP_HOPS, 2, CUT, width), BF),
            vmem((DOWN_HOPS, 2, CUT, width), BF),
            vmem((DOWN_HOPS, 2, CUT, width), BF),
            vmem((SLOTS, width), F32),
            vmem((width // HD * SLOTS, nbytes), F32),
            dma((4,)), dma((7, 3)), dma((SIDE, 2, 3)), dma((3,)), dma((2,)),
            dma((SIDE, 4)), dma((SIDE, 4)), dma((SIDE, 4)),
            dma((2, 3)), dma((2, 3)), dma((62,)), dma((2, 2, SIDE, SIDE)),
            dma((NZ, 2)), dma((NZ, 2)), dma((NZ, 2)),
            dma((NZ,)), dma((NZ,)),
            dma((UP_HOPS, 2)), dma((UP_HOPS, 2)), dma((DOWN_HOPS, 2)), dma((DOWN_HOPS, 2)),
        ],
        compiler_params=pltpu.CompilerParams(
            collective_id=0, has_side_effects=True, vmem_limit_bytes=60 * 1024 * 1024
        ),
    )(
        enc_states, dec_states, segments.reshape(1, nbytes), patch_keys, w_in,
        w_gate.T, w_up.T, w_down, w_out,
    )
    return (dec_states.astype(F32) + mixed).astype(BF)


def solution(mesh):
    placed = (
        P(("seq", "mp"), None),
        P(("seq", "mp"), None),
        P(("seq", "mp")),
        P(("seq", "mp"), None),
        P(None, "mp"),
        P("seq", "mp"),
        P("seq", "mp"),
        P("mp", "seq"),
        P("mp", None),
    )
    return jax.shard_map(
        body, mesh=mesh, in_specs=placed, out_specs=P(("seq", "mp"), None), check_vma=False
    )
```

```python
import math

import jax
import jax.numpy as jnp
from jax import lax
from jax.experimental import pallas as pl
from jax.experimental.pallas import tpu as pltpu
from jax.sharding import PartitionSpec as P

MESH = pl.DeviceIdType.MESH
HD = 128
SIDE = 4
NZ = 16
SLOTS = 32
CUT = SLOTS // 2
CHUNKS = 4
BF = jnp.bfloat16
F32 = jnp.float32
EPS = 1e-05
NT = (((1,), (1,)), ((), ()))
UP_HOPS = 8
DOWN_HOPS = 7
PAD = 512
LANES = (2 * PAD // SIDE, PAD // SIDE)


def mm(a, b):
    return jnp.dot(a, b, preferred_element_type=F32)


def mm_nt(a, b):
    return lax.dot_general(a, b, NT, preferred_element_type=F32)


def kernel(
    enc_hbm, dec_hbm, seg_ref, keys_ref, win_hbm, wg_hbm, wu_hbm, wd_hbm, wout_hbm,
    out_ref,
    enc_ref, dec_ref, win_ref, wout_ref,
    rg, ru, rd, bc, ug, ud, rsg, rsd, wf, pall, st, rc, xs, ob, rzp, szp, rzm, szm, kpad, wts,
    in_s, raw_s, raw_r, loc_s, src_s, bc_r, bc_sp, bc_sm, rs_s, rs_r, w_s, w_r, h_r,
    p_r, p_sp, p_sm, st_r, st_s, zp_s, zp_r, zm_s, zm_r,
):
    s = lax.axis_index("seq")
    z = lax.axis_index("mp")
    k = s % 2
    x = (s // 2) % SIDE
    y = s // (2 * SIDE)
    a = x + k * (y - x)
    b = y + k * (x - y)
    width = enc_ref.shape[1]
    half = width // 2
    quarter = half // SIDE
    eighth = quarter // 2
    units = wg_hbm.shape[0]

    def dev(xx, yy, kk, zz):
        return {"seq": (yy * SIDE + xx) * 2 + kk, "mp": zz}

    def x_peer(j, kk):
        return dev((x + j) % SIDE, y, kk, z)

    def y_peer(j, kk):
        return dev(x, (y + j) % SIDE, kk, z)

    def a_peer(j):
        return dev((x + j * (1 - k)) % SIDE, (y + j * k) % SIDE, k, z)

    def b_peer(j):
        return dev((x + j * k) % SIDE, (y + j * (1 - k)) % SIDE, k, z)

    def z_peer(j):
        return dev(x, y, k, (z + j) % NZ)

    partner = dev(x, y, 1 - k, z)
    above = z_peer(1)
    below = z_peer(NZ - 1)

    barrier = pltpu.get_barrier_semaphore()
    greeted = [above, below, partner]
    for j in (2, 1, 3):
        for kk in (0, 1):
            greeted += [x_peer(j, kk), y_peer(j, kk)]
    for d in greeted:
        pl.semaphore_signal(barrier, inc=1, device_id=d, device_id_type=MESH)

    def remote(src, dst, ssem, rsem, d):
        return pltpu.make_async_remote_copy(
            src_ref=src, dst_ref=dst, send_sem=ssem, recv_sem=rsem, device_id=d, device_id_type=MESH
        )

    loads = []
    for i, (src, dst) in enumerate(
        ((wout_hbm, wout_ref), (enc_hbm, enc_ref), (win_hbm, win_ref), (dec_hbm, dec_ref))
    ):
        c = pltpu.make_async_copy(src, dst, in_s.at[i])
        c.start()
        loads.append(c)

    def source(zz):
        hit0 = (zz // SIDE) == y
        hit1 = (zz % SIDE) == x
        hit = jnp.where(k == 0, hit0, hit1)
        slot = jnp.where(k == 0, zz % SIDE, zz // SIDE)
        return hit, slot

    first_row = k * half + a * quarter
    hit_me, slot_me = source(z)

    def src_copy(h):
        row = pl.multiple_of(first_row + h * eighth, 16)
        return pltpu.make_async_copy(win_hbm.at[pl.ds(row, eighth), :], bc.at[slot_me, h], src_s.at[h])

    @pl.when(hit_me)
    def _():
        src_copy(0).start()
        src_copy(1).start()

    raws = ((wg_hbm, rg), (wu_hbm, ru), (wd_hbm, rd))
    raw_local = []
    for i, (src, dst) in enumerate(raws):
        c = pltpu.make_async_copy(src, dst.at[a, k], loc_s.at[i])
        c.start()
        raw_local.append(c)

    pl.semaphore_wait(barrier, len(greeted))

    def bc_send(slot, part, up):
        sems = bc_sp if up else bc_sm
        return remote(
            bc.at[slot, part], bc.at[slot, part], sems.at[slot, part], bc_r.at[slot, part],
            above if up else below,
        )

    @pl.when(hit_me)
    def _():
        for h in (0, 1):
            src_copy(h).wait()
            bc_send(slot_me, h, True).start()
            bc_send(slot_me, h, False).start()

    raw_targets = [(partner, b)]
    for j in (1, 3, 2):
        raw_targets += [(x_peer(j, 0), x), (y_peer(j, 1), y)]
    raw_sends = []
    for i, (src, dst) in enumerate(raws):
        for n, (d, slot) in enumerate(raw_targets):
            c = remote(src, dst.at[slot, k], raw_s.at[n, i], raw_r.at[slot, k, i], d)
            c.start()
            raw_sends.append(c)

    loads[0].wait()

    @pl.when(hit_me)
    def _():
        rows = lax.broadcasted_iota(jnp.int32, (quarter, width), 0) + first_row
        cols = lax.broadcasted_iota(jnp.int32, (quarter, width), 1)
        pick = jnp.where(rows == cols, 1.0, 0.0).astype(BF)
        turned = mm_nt(pick, wout_ref[...]).astype(BF)
        for h in (0, 1):
            bc[slot_me, 2 + h] = turned[h * eighth : (h + 1) * eighth]
            bc_send(slot_me, 2 + h, True).start()
            bc_send(slot_me, 2 + h, False).start()

    def bc_step(t, parts):
        if not 1 <= t <= UP_HOPS:
            return
        hit_u, slot_u = source((z + NZ - t) % NZ)
        hit_d, slot_d = source((z + t) % NZ)
        for part in parts:

            @pl.when(hit_u)
            def _():
                bc_send(slot_u, part, True).wait_recv()
                if t < UP_HOPS:
                    bc_send(slot_u, part, True).start()

            if t <= DOWN_HOPS:

                @pl.when(hit_d)
                def _():
                    bc_send(slot_d, part, False).wait_recv()
                    if t < DOWN_HOPS:
                        bc_send(slot_d, part, False).start()

    loads[1].wait()
    member = lax.broadcasted_iota(jnp.int32, (SLOTS, enc_ref.shape[0]), 0) == seg_ref[...]
    member = jnp.where(member, 1.0, 0.0)
    lengths = jnp.maximum(jnp.sum(member, axis=1, keepdims=True), 1.0)
    pall[z] = (mm(member.astype(BF), enc_ref[...]) / lengths).astype(BF)

    def p_send(slot, h, up):
        view = pall.at[slot, pl.ds(h // 2 * CUT, CUT), pl.ds(h % 2 * half, half)]
        ssem = p_sp if up else p_sm
        return remote(view, view, ssem.at[slot, h], p_r.at[slot, h], above if up else below)

    def p_step(t):
        if not 0 <= t <= UP_HOPS:
            return
        up_slot = (z + NZ - t) % NZ
        down_slot = (z + t) % NZ
        for h in range(CHUNKS):
            if t:
                p_send(up_slot, h, True).wait_recv()
            if t < UP_HOPS:
                p_send(up_slot, h, True).start()
            if 1 <= t <= DOWN_HOPS:
                p_send(down_slot, h, False).wait_recv()
            if t < DOWN_HOPS:
                p_send(down_slot, h, False).start()

    ug[...] = jnp.zeros_like(ug)
    ud[...] = jnp.zeros_like(ud)
    lag = 4
    for t in range(1, UP_HOPS + 1):
        bc_step(t, (0, 1))
        bc_step(t - 1, (2, 3))
        p_step(t - lag)

    def raw_wait(i):
        raw_local[i].wait()
        src, dst = raws[i]
        for d in range(SIDE):
            for kk in (0, 1):

                @pl.when(jnp.logical_or(a != d, k != kk))
                def _():
                    remote(src, dst.at[d, kk], raw_s.at[0, 0], raw_r.at[d, kk, i], partner).wait_recv()

    def deep(buf):
        return jnp.concatenate([buf[i, kk] for i in range(SIDE) for kk in (0, 1)], axis=1)

    def tall(part):
        return jnp.concatenate(
            [jnp.concatenate([bc[i, part + h] for i in range(SIDE)], axis=1) for h in (0, 1)], axis=0
        )

    rs_copies = [[], []]

    def piece(part, bb, base=0):
        return pl.ds(pl.multiple_of(base + bb * LANES[part], 128), LANES[part])

    def rs_send(part):
        src, dst = ((ug, rsg), (ud, rsd))[part]
        for j in (2, 1, 3):
            c = remote(
                src.at[:, piece(part, (b + j) % SIDE)], dst.at[j - 1],
                rs_s.at[part, j - 1], rs_r.at[part, j - 1], b_peer(j),
            )
            c.start()
            rs_copies[part].append(c)

    raw_wait(0)
    raw_wait(1)
    ins = tall(0)
    ug[:, 0:units] = mm_nt(ins, deep(rg)).astype(BF)
    ug[:, PAD : PAD + units] = mm_nt(ins, deep(ru)).astype(BF)
    rs_send(0)
    bc_step(UP_HOPS, (2, 3))
    p_step(UP_HOPS - lag + 1)
    raw_wait(2)
    ud[:, 0:units] = mm_nt(tall(2), deep(rd)).astype(BF)
    rs_send(1)
    p_step(UP_HOPS - lag + 2)

    def place(part, kk, aa, bb):
        row = pl.multiple_of(kk * half + aa * quarter, 32)
        return wf.at[pl.ds(row, quarter), piece(part, bb, part * 2 * PAD)]

    w_copies = []

    def w_send(part, kk, aa, bb, d):
        n = len(w_copies)
        view = place(part, kk, aa, bb)
        c = remote(view, view, w_s.at[n], w_r.at[part, kk, aa, bb], d)
        c.start()
        w_copies.append(c)

    def w_half(part, aa, bb, h):
        row = pl.multiple_of(k * half + aa * quarter + h * eighth, 16)
        return wf.at[pl.ds(row, eighth), piece(part, bb, part * 2 * PAD)]

    def w_relay(part, aa, bb, h, d):
        n = len(w_copies)
        view = w_half(part, aa, bb, h)
        c = remote(view, view, w_s.at[n], h_r.at[part, bb, h], d)
        c.start()
        w_copies.append(c)

    def w_wait(part, kk, aa, bb):
        view = place(part, kk, aa, bb)
        remote(view, view, w_s.at[0], w_r.at[part, kk, aa, bb], partner).wait_recv()

    def w_sum(part):
        src, got = ((ug, rsg), (ud, rsd))[part]
        total = src[:, piece(part, b)].astype(F32)
        for c in rs_copies[part]:
            c.wait_recv()
        for j in (0, 1, 2):
            total += got[j].astype(F32)
        place(part, k, a, b)[...] = total.astype(BF)
        for j in (2, 1, 3):
            w_send(part, k, a, b, b_peer(j))
        for j in (1, 3):
            w_send(part, k, a, b, a_peer(j))
        w_send(part, k, a, b, partner)

    def w_pass(part):
        for j in (1, 3, 2):
            bb = (b + j) % SIDE
            w_wait(part, k, a, bb)
            for i in (1, 3):
                w_send(part, k, a, bb, a_peer(i))
            w_send(part, k, a, bb, partner)

    w_sum(0)
    p_step(UP_HOPS - lag + 3)
    w_sum(1)
    p_step(UP_HOPS - lag + 4)
    w_pass(0)

    loads[2].wait()
    rows = NZ * SLOTS
    for lo in range(0, NZ, 4):
        pr = pall[lo : lo + 4].reshape(4 * SLOTS, width)
        xr = mm(pr, win_ref[...]).astype(BF)
        xs[lo * SLOTS : (lo + 4) * SLOTS, :] = xr
        sq = xr.astype(F32)
        sq = sq * sq
        sq = sq[:, 0:128] + sq[:, 128:256]
        st[z, :, lo * SLOTS : (lo + 4) * SLOTS] = jnp.sum(jnp.transpose(sq), axis=0, keepdims=True)
    st_copies = []
    for j in (8, 7, 9, 6, 10, 5, 11, 4, 12, 3, 13, 2, 14, 1, 15):
        c = remote(st.at[z], st.at[z], st_s.at[j], st_r.at[z], z_peer(j))
        c.start()
        st_copies.append(c)
    w_pass(1)
    for lo in range(0, rows, 4 * SLOTS):
        ob[lo : lo + 4 * SLOTS, :] = mm(xs[lo : lo + 4 * SLOTS, :], wout_ref[...])

    loads[3].wait()
    heads = width // HD
    kpad[...] = jnp.zeros_like(kpad)
    kpad[0 : keys_ref.shape[0], :] = keys_ref[...].astype(F32)
    own = lax.broadcasted_iota(jnp.int32, (heads * SLOTS, width), 0) // SLOTS
    own = own == lax.broadcasted_iota(jnp.int32, (heads * SLOTS, width), 1) // HD
    kb = jnp.where(own, jnp.concatenate([kpad[...]] * heads, axis=0), 0.0).astype(BF)
    scores = mm_nt(kb, dec_ref[...]) / math.sqrt(HD)
    allowed = lax.broadcasted_iota(jnp.int32, (SLOTS, dec_ref.shape[0]), 0) <= seg_ref[...]
    for h in range(heads):
        sc = jnp.where(allowed, scores[h * SLOTS : (h + 1) * SLOTS], -1e30)
        ex = jnp.exp(sc - jnp.max(sc, axis=0, keepdims=True))
        wts[h * SLOTS : (h + 1) * SLOTS, :] = ex / jnp.sum(ex, axis=0, keepdims=True)
    wt = jnp.transpose(wts[...]).astype(BF)

    for part in (0, 1):
        for i in (0, 1, 3, 2):
            bb = (b + i) % SIDE
            for j in (1, 3):
                aa = (a + j) % SIDE
                w_wait(part, k, aa, bb)
                w_relay(part, aa, bb, j // 2, a_peer(SIDE - j))
                w_send(part, k, aa, bb, partner)
        for i in (0, 1, 3, 2):
            bb = (b + i) % SIDE
            aa = (a + 2) % SIDE
            for h in (0, 1):
                view = w_half(part, aa, bb, h)
                remote(view, view, w_s.at[0], h_r.at[part, bb, h], partner).wait_recv()
            w_send(part, k, aa, bb, partner)

    for j in range(1, NZ):
        slot = (z + j) % NZ
        remote(st.at[slot], st.at[slot], st_s.at[0], st_r.at[slot], above).wait_recv()
    stat = st[0]
    for i in range(1, NZ):
        stat += st[i]
    inv = lax.rsqrt(stat / (NZ * win_ref.shape[1]) + EPS)
    for i in range(0, NZ, 4):
        r = jnp.transpose(jnp.broadcast_to(inv[:, i * SLOTS : (i + 4) * SLOTS], (HD, 4 * SLOTS)))
        rc[i : i + 4] = r.reshape(4, SLOTS, HD)

    for part in (0, 1):
        for aa in range(SIDE):
            for bb in range(SIDE):
                w_wait(part, 1 - k, aa, bb)

    def ffn(t):
        d1 = (z + UP_HOPS - t) % NZ
        d2 = (z + NZ - DOWN_HOPS + t) % NZ
        pr = jnp.concatenate([pall[d1], pall[d2]], axis=0)
        r = jnp.concatenate([rc[d1], rc[d2]], axis=0)
        r = jnp.concatenate([r] * (PAD // HD), axis=1)
        g = mm(pr, wf[:, 0:PAD]) * r
        u = mm(pr, wf[:, PAD : 2 * PAD]) * r
        hid = (g / (1.0 + jnp.exp(-g)) * u).astype(BF)
        o = mm_nt(hid, wf[:, 2 * PAD : 3 * PAD])
        row1 = pl.multiple_of(d1 * SLOTS, SLOTS)
        row2 = pl.multiple_of(d2 * SLOTS, SLOTS)
        return (
            o[0:SLOTS] + ob[pl.ds(row1, SLOTS), :],
            o[SLOTS : 2 * SLOTS] + ob[pl.ds(row2, SLOTS), :],
        )

    def chunk(val, h):
        return val[h // 2 * CUT : (h // 2 + 1) * CUT, h % 2 * half : (h % 2 + 1) * half]

    zp_copies, zm_copies = {}, {}
    for t in range(UP_HOPS):
        up_val, down_val = ffn(t)
        for h in range(CHUNKS):
            val = chunk(up_val, h)
            if t:
                zp_copies[t - 1, h].wait_recv()
                val += rzp[t - 1, h].astype(F32)
            szp[t, h] = val.astype(BF)
            c = remote(szp.at[t, h], rzp.at[t, h], zp_s.at[t, h], zp_r.at[t, h], above)
            c.start()
            zp_copies[t, h] = c
            if t < DOWN_HOPS:
                val = chunk(down_val, h)
                if t:
                    zm_copies[t - 1, h].wait_recv()
                    val += rzm[t - 1, h].astype(F32)
                szm[t, h] = val.astype(BF)
                c = remote(szm.at[t, h], rzm.at[t, h], zm_s.at[t, h], zm_r.at[t, h], below)
                c.start()
                zm_copies[t, h] = c

    vals = []
    for h in range(CHUNKS):
        zm_copies[DOWN_HOPS - 1, h].wait_recv()
        val = chunk(down_val, h) + rzm[DOWN_HOPS - 1, h].astype(F32)
        zp_copies[UP_HOPS - 1, h].wait_recv()
        vals.append(val + rzp[UP_HOPS - 1, h].astype(F32))
    values = jnp.concatenate(
        [jnp.concatenate(vals[i : i + 2], axis=1) for i in (0, 2)], axis=0
    )
    vb = jnp.where(own, jnp.concatenate([values] * heads, axis=0), 0.0).astype(BF)
    out_ref[...] = mm(wt, vb)

    for c in raw_sends + rs_copies[0] + rs_copies[1] + w_copies + st_copies:
        c.wait_send()
    for i in range(SIDE):
        zi = jnp.where(k == 0, SIDE * y + i, SIDE * i + x)
        up_dist = (z - zi + NZ) % NZ
        down_dist = (zi - z + NZ) % NZ
        for part in range(4):

            @pl.when(up_dist < UP_HOPS)
            def _():
                bc_send(i, part, True).wait_send()

            @pl.when(down_dist < DOWN_HOPS)
            def _():
                bc_send(i, part, False).wait_send()

    for h in range(CHUNKS):
        for t in range(UP_HOPS):
            p_send((z + NZ - t) % NZ, h, True).wait_send()
        for t in range(DOWN_HOPS):
            p_send((z + t) % NZ, h, False).wait_send()
    for c in (*zp_copies.values(), *zm_copies.values()):
        c.wait_send()


def body(enc_states, dec_states, segments, patch_keys, w_in, w_gate, w_up, w_down, w_out):
    nbytes, width = enc_states.shape
    depth, units = w_gate.shape
    local = w_in.shape[1]
    quarter = width // 8
    rows = NZ * SLOTS
    dma = pltpu.SemaphoreType.DMA
    vmem = pltpu.VMEM
    hbm = pl.BlockSpec(memory_space=pl.ANY)
    here = pl.BlockSpec(memory_space=pltpu.VMEM)
    mixed = pl.pallas_call(
        kernel,
        out_shape=jax.ShapeDtypeStruct((nbytes, width), F32),
        in_specs=[hbm, hbm, here, here, hbm, hbm, hbm, hbm, hbm],
        out_specs=here,
        scratch_shapes=[
            vmem((nbytes, width), BF),
            vmem((nbytes, width), BF),
            vmem((width, local), BF),
            vmem((local, width), BF),
            vmem((SIDE, 2, units, depth), BF),
            vmem((SIDE, 2, units, depth), BF),
            vmem((SIDE, 2, units, depth), BF),
            vmem((SIDE, 4, quarter // 2, local), BF),
            vmem((quarter, 2 * PAD), BF),
            vmem((quarter, PAD), BF),
            vmem((3, quarter, LANES[0]), BF),
            vmem((3, quarter, LANES[1]), BF),
            vmem((width, 3 * PAD), BF),
            vmem((NZ, SLOTS, width), BF),
            vmem((NZ, 1, rows), F32),
            vmem((NZ, SLOTS, HD), F32),
            vmem((rows, local), BF),
            vmem((rows, width), F32),
            vmem((UP_HOPS, CHUNKS, CUT, width // 2), BF),
            vmem((UP_HOPS, CHUNKS, CUT, width // 2), BF),
            vmem((DOWN_HOPS, CHUNKS, CUT, width // 2), BF),
            vmem((DOWN_HOPS, CHUNKS, CUT, width // 2), BF),
            vmem((SLOTS, width), F32),
            vmem((width // HD * SLOTS, nbytes), F32),
            dma((4,)), dma((7, 3)), dma((SIDE, 2, 3)), dma((3,)), dma((2,)),
            dma((SIDE, 4)), dma((SIDE, 4)), dma((SIDE, 4)),
            dma((2, 3)), dma((2, 3)), dma((72,)), dma((2, 2, SIDE, SIDE)), dma((2, SIDE, 2)),
            dma((NZ, CHUNKS)), dma((NZ, CHUNKS)), dma((NZ, CHUNKS)),
            dma((NZ,)), dma((NZ,)),
            dma((UP_HOPS, CHUNKS)), dma((UP_HOPS, CHUNKS)), dma((DOWN_HOPS, CHUNKS)), dma((DOWN_HOPS, CHUNKS)),
        ],
        compiler_params=pltpu.CompilerParams(
            collective_id=0, has_side_effects=True, vmem_limit_bytes=60 * 1024 * 1024
        ),
    )(
        enc_states, dec_states, segments.reshape(1, nbytes), patch_keys, w_in,
        w_gate.T, w_up.T, w_down, w_out,
    )
    return (dec_states.astype(F32) + mixed).astype(BF)


def solution(mesh):
    placed = (
        P(("seq", "mp"), None),
        P(("seq", "mp"), None),
        P(("seq", "mp")),
        P(("seq", "mp"), None),
        P(None, "mp"),
        P("seq", "mp"),
        P("seq", "mp"),
        P("mp", "seq"),
        P("mp", None),
    )
    return jax.shard_map(
        body, mesh=mesh, in_specs=placed, out_specs=P(("seq", "mp"), None), check_vma=False
    )
```

```python
import math

import jax
import jax.numpy as jnp
from jax import lax
from jax.experimental import pallas as pl
from jax.experimental.pallas import tpu as pltpu
from jax.sharding import PartitionSpec as P

MESH = pl.DeviceIdType.MESH
HD = 128
SIDE = 4
NZ = 16
SLOTS = 32
CUT = SLOTS // 2
BF = jnp.bfloat16
F32 = jnp.float32
EPS = 1e-05
NT = (((1,), (1,)), ((), ()))
UP_HOPS = 8
DOWN_HOPS = 7
PAD = 512
LANES = (2 * PAD // SIDE, PAD // SIDE)


def mm(a, b):
    return jnp.dot(a, b, preferred_element_type=F32)


def mm_nt(a, b):
    return lax.dot_general(a, b, NT, preferred_element_type=F32)


def kernel(
    enc_hbm, dec_hbm, seg_ref, keys_ref, win_hbm, wg_hbm, wu_hbm, wd_hbm, wout_hbm,
    out_ref,
    enc_ref, dec_ref, win_ref, wout_ref,
    rg, ru, rd, bc, ug, ud, rsg, rsd, wf, pall, st, rc, xs, ob, rzp, szp, rzm, szm, kpad, wts,
    in_s, raw_s, raw_r, loc_s, src_s, bc_r, bc_sp, bc_sm, rs_s, rs_r, w_s, w_r,
    p_r, p_sp, p_sm, st_r, st_s, zp_s, zp_r, zm_s, zm_r,
):
    s = lax.axis_index("seq")
    z = lax.axis_index("mp")
    k = s % 2
    x = (s // 2) % SIDE
    y = s // (2 * SIDE)
    a = x + k * (y - x)
    b = y + k * (x - y)
    width = enc_ref.shape[1]
    half = width // 2
    quarter = half // SIDE
    eighth = quarter // 2
    units = wg_hbm.shape[0]

    def dev(xx, yy, kk, zz):
        return {"seq": (yy * SIDE + xx) * 2 + kk, "mp": zz}

    def x_peer(j, kk):
        return dev((x + j) % SIDE, y, kk, z)

    def y_peer(j, kk):
        return dev(x, (y + j) % SIDE, kk, z)

    def a_peer(j):
        return dev((x + j * (1 - k)) % SIDE, (y + j * k) % SIDE, k, z)

    def b_peer(j):
        return dev((x + j * k) % SIDE, (y + j * (1 - k)) % SIDE, k, z)

    def z_peer(j):
        return dev(x, y, k, (z + j) % NZ)

    partner = dev(x, y, 1 - k, z)
    above = z_peer(1)
    below = z_peer(NZ - 1)

    barrier = pltpu.get_barrier_semaphore()
    above2 = z_peer(2)
    below2 = z_peer(NZ - 2)
    greeted = [above2, below2, above, below, partner]
    for j in (2, 1, 3):
        for kk in (0, 1):
            greeted += [x_peer(j, kk), y_peer(j, kk)]
    for d in greeted:
        pl.semaphore_signal(barrier, inc=1, device_id=d, device_id_type=MESH)

    def remote(src, dst, ssem, rsem, d):
        return pltpu.make_async_remote_copy(
            src_ref=src, dst_ref=dst, send_sem=ssem, recv_sem=rsem, device_id=d, device_id_type=MESH
        )

    loads = []
    for i, (src, dst) in enumerate(
        ((wout_hbm, wout_ref), (enc_hbm, enc_ref), (win_hbm, win_ref), (dec_hbm, dec_ref))
    ):
        c = pltpu.make_async_copy(src, dst, in_s.at[i])
        c.start()
        loads.append(c)

    def source(zz):
        hit0 = (zz // SIDE) == y
        hit1 = (zz % SIDE) == x
        hit = jnp.where(k == 0, hit0, hit1)
        slot = jnp.where(k == 0, zz % SIDE, zz // SIDE)
        return hit, slot

    first_row = k * half + a * quarter
    hit_me, slot_me = source(z)

    def src_copy(h):
        row = pl.multiple_of(first_row + h * eighth, 16)
        return pltpu.make_async_copy(win_hbm.at[pl.ds(row, eighth), :], bc.at[slot_me, h], src_s.at[h])

    @pl.when(hit_me)
    def _():
        src_copy(0).start()
        src_copy(1).start()

    raws = ((wg_hbm, rg), (wu_hbm, ru), (wd_hbm, rd))
    raw_local = []
    for i, (src, dst) in enumerate(raws):
        c = pltpu.make_async_copy(src, dst.at[a, k], loc_s.at[i])
        c.start()
        raw_local.append(c)

    pl.semaphore_wait(barrier, len(greeted))

    def bc_send(slot, part, up, far=0):
        sems = bc_sp if up else bc_sm
        target = ((below, below2), (above, above2))[up][far]
        view = bc.at[slot, part]
        return remote(view, view, sems.at[slot, part, far], bc_r.at[slot, part], target)

    def bc_spread(slot, part, up, far=True):
        if far:
            bc_send(slot, part, up, 1).start()
        bc_send(slot, part, up, 0).start()

    @pl.when(hit_me)
    def _():
        for h in (0, 1):
            src_copy(h).wait()
            bc_spread(slot_me, h, True)
            bc_spread(slot_me, h, False)

    raw_targets = [(partner, b)]
    for j in (1, 3, 2):
        raw_targets += [(x_peer(j, 0), x), (y_peer(j, 1), y)]
    raw_sends = []
    for i, (src, dst) in enumerate(raws):
        for n, (d, slot) in enumerate(raw_targets):
            c = remote(src, dst.at[slot, k], raw_s.at[n, i], raw_r.at[slot, k, i], d)
            c.start()
            raw_sends.append(c)

    loads[0].wait()

    @pl.when(hit_me)
    def _():
        rows = lax.broadcasted_iota(jnp.int32, (quarter, width), 0) + first_row
        cols = lax.broadcasted_iota(jnp.int32, (quarter, width), 1)
        pick = jnp.where(rows == cols, 1.0, 0.0).astype(BF)
        turned = mm_nt(pick, wout_ref[...]).astype(BF)
        for h in (0, 1):
            bc[slot_me, 2 + h] = turned[h * eighth : (h + 1) * eighth]
            bc_spread(slot_me, 2 + h, True)
            bc_spread(slot_me, 2 + h, False)

    def bc_step(t, parts):
        if not 1 <= t <= UP_HOPS // 2:
            return
        for dist in (2 * t, 2 * t - 1):
            hit_u, slot_u = source((z + NZ - dist) % NZ)
            hit_d, slot_d = source((z + dist) % NZ)
            for part in parts:

                @pl.when(hit_u)
                def _():
                    bc_send(slot_u, part, True).wait_recv()
                    if dist % 2 == 0 and dist < UP_HOPS:
                        bc_spread(slot_u, part, True)

                if dist <= DOWN_HOPS:

                    @pl.when(hit_d)
                    def _():
                        bc_send(slot_d, part, False).wait_recv()
                        if dist % 2 == 0 and dist < DOWN_HOPS:
                            bc_spread(slot_d, part, False, dist + 2 <= DOWN_HOPS)

    loads[1].wait()
    member = lax.broadcasted_iota(jnp.int32, (SLOTS, enc_ref.shape[0]), 0) == seg_ref[...]
    member = jnp.where(member, 1.0, 0.0)
    lengths = jnp.maximum(jnp.sum(member, axis=1, keepdims=True), 1.0)
    pall[z] = (mm(member.astype(BF), enc_ref[...]) / lengths).astype(BF)

    def p_send(slot, h, up):
        view = pall.at[slot, pl.ds(h * CUT, CUT), :]
        ssem = p_sp if up else p_sm
        return remote(view, view, ssem.at[slot, h], p_r.at[slot, h], above if up else below)

    def p_step(t):
        if not 0 <= t <= UP_HOPS:
            return
        up_slot = (z + NZ - t) % NZ
        down_slot = (z + t) % NZ
        for h in (0, 1):
            if t:
                p_send(up_slot, h, True).wait_recv()
            if t < UP_HOPS:
                p_send(up_slot, h, True).start()
            if 1 <= t <= DOWN_HOPS:
                p_send(down_slot, h, False).wait_recv()
            if t < DOWN_HOPS:
                p_send(down_slot, h, False).start()

    ug[...] = jnp.zeros_like(ug)
    ud[...] = jnp.zeros_like(ud)
    p_step(0)
    for t in range(1, 5):
        bc_step(t, (0, 1))
        p_step(t)
        bc_step(t - 1, (2, 3))

    def raw_wait(i):
        raw_local[i].wait()
        src, dst = raws[i]
        for d in range(SIDE):
            for kk in (0, 1):

                @pl.when(jnp.logical_or(a != d, k != kk))
                def _():
                    remote(src, dst.at[d, kk], raw_s.at[0, 0], raw_r.at[d, kk, i], partner).wait_recv()

    def deep(buf):
        return jnp.concatenate([buf[i, kk] for i in range(SIDE) for kk in (0, 1)], axis=1)

    def tall(part):
        return jnp.concatenate(
            [jnp.concatenate([bc[i, part + h] for i in range(SIDE)], axis=1) for h in (0, 1)], axis=0
        )

    rs_copies = [[], []]

    def piece(part, bb, base=0):
        return pl.ds(pl.multiple_of(base + bb * LANES[part], 128), LANES[part])

    def rs_send(part):
        src, dst = ((ug, rsg), (ud, rsd))[part]
        for j in (2, 1, 3):
            c = remote(
                src.at[:, piece(part, (b + j) % SIDE)], dst.at[j - 1],
                rs_s.at[part, j - 1], rs_r.at[part, j - 1], b_peer(j),
            )
            c.start()
            rs_copies[part].append(c)

    raw_wait(0)
    raw_wait(1)
    ins = tall(0)
    ug[:, 0:units] = mm_nt(ins, deep(rg)).astype(BF)
    ug[:, PAD : PAD + units] = mm_nt(ins, deep(ru)).astype(BF)
    rs_send(0)
    bc_step(4, (2, 3))
    p_step(5)
    raw_wait(2)
    ud[:, 0:units] = mm_nt(tall(2), deep(rd)).astype(BF)
    rs_send(1)

    def place(part, kk, aa, bb):
        row = pl.multiple_of(kk * half + aa * quarter, 32)
        return wf.at[pl.ds(row, quarter), piece(part, bb, part * 2 * PAD)]

    w_copies = []

    def w_send(part, kk, aa, bb, d):
        n = len(w_copies)
        view = place(part, kk, aa, bb)
        c = remote(view, view, w_s.at[n], w_r.at[part, kk, aa, bb], d)
        c.start()
        w_copies.append(c)

    def w_wait(part, kk, aa, bb):
        view = place(part, kk, aa, bb)
        remote(view, view, w_s.at[0], w_r.at[part, kk, aa, bb], partner).wait_recv()

    def w_sum(part):
        src, got = ((ug, rsg), (ud, rsd))[part]
        total = src[:, piece(part, b)].astype(F32)
        for c in rs_copies[part]:
            c.wait_recv()
        for j in (0, 1, 2):
            total += got[j].astype(F32)
        place(part, k, a, b)[...] = total.astype(BF)
        for j in (2, 1, 3):
            w_send(part, k, a, b, b_peer(j))
        for j in (2, 1, 3):
            w_send(part, k, a, b, a_peer(j))
        w_send(part, k, a, b, partner)

    def w_pass(part):
        for j in (1, 3, 2):
            bb = (b + j) % SIDE
            w_wait(part, k, a, bb)
            for i in (2, 1, 3):
                w_send(part, k, a, bb, a_peer(i))
            w_send(part, k, a, bb, partner)

    w_sum(0)
    p_step(6)
    w_sum(1)
    w_pass(0)
    p_step(7)
    w_pass(1)
    p_step(8)

    loads[2].wait()
    rows = NZ * SLOTS
    for lo in range(0, NZ, 4):
        pr = pall[lo : lo + 4].reshape(4 * SLOTS, width)
        xr = mm(pr, win_ref[...]).astype(BF)
        xs[lo * SLOTS : (lo + 4) * SLOTS, :] = xr
        sq = xr.astype(F32)
        sq = sq * sq
        sq = sq[:, 0:128] + sq[:, 128:256]
        st[z, :, lo * SLOTS : (lo + 4) * SLOTS] = jnp.sum(jnp.transpose(sq), axis=0, keepdims=True)
    st_copies = []
    for j in (8, 7, 9, 6, 10, 5, 11, 4, 12, 3, 13, 2, 14, 1, 15):
        c = remote(st.at[z], st.at[z], st_s.at[j], st_r.at[z], z_peer(j))
        c.start()
        st_copies.append(c)
    for lo in range(0, rows, 4 * SLOTS):
        ob[lo : lo + 4 * SLOTS, :] = mm(xs[lo : lo + 4 * SLOTS, :], wout_ref[...])

    loads[3].wait()
    heads = width // HD
    kpad[...] = jnp.zeros_like(kpad)
    kpad[0 : keys_ref.shape[0], :] = keys_ref[...].astype(F32)
    own = lax.broadcasted_iota(jnp.int32, (heads * SLOTS, width), 0) // SLOTS
    own = own == lax.broadcasted_iota(jnp.int32, (heads * SLOTS, width), 1) // HD
    kb = jnp.where(own, jnp.concatenate([kpad[...]] * heads, axis=0), 0.0).astype(BF)
    scores = mm_nt(kb, dec_ref[...]) / math.sqrt(HD)
    allowed = lax.broadcasted_iota(jnp.int32, (SLOTS, dec_ref.shape[0]), 0) <= seg_ref[...]
    for h in range(heads):
        sc = jnp.where(allowed, scores[h * SLOTS : (h + 1) * SLOTS], -1e30)
        ex = jnp.exp(sc - jnp.max(sc, axis=0, keepdims=True))
        wts[h * SLOTS : (h + 1) * SLOTS, :] = ex / jnp.sum(ex, axis=0, keepdims=True)
    wt = jnp.transpose(wts[...]).astype(BF)

    for part in (0, 1):
        for j in (1, 3, 2):
            aa = (a + j) % SIDE
            for i in (0, 1, 3, 2):
                bb = (b + i) % SIDE
                w_wait(part, k, aa, bb)
                w_send(part, k, aa, bb, partner)

    for j in range(1, NZ):
        slot = (z + j) % NZ
        remote(st.at[slot], st.at[slot], st_s.at[0], st_r.at[slot], above).wait_recv()
    stat = st[0]
    for i in range(1, NZ):
        stat += st[i]
    inv = lax.rsqrt(stat / (NZ * win_ref.shape[1]) + EPS)
    for i in range(0, NZ, 4):
        r = jnp.transpose(jnp.broadcast_to(inv[:, i * SLOTS : (i + 4) * SLOTS], (HD, 4 * SLOTS)))
        rc[i : i + 4] = r.reshape(4, SLOTS, HD)

    for part in (0, 1):
        for aa in range(SIDE):
            for bb in range(SIDE):
                w_wait(part, 1 - k, aa, bb)

    def ffn(dests):
        pr = jnp.concatenate([pall[d] for d in dests], axis=0)
        r = jnp.concatenate([rc[d] for d in dests], axis=0)
        r = jnp.concatenate([r] * (PAD // HD), axis=1)
        g = mm(pr, wf[:, 0:PAD]) * r
        u = mm(pr, wf[:, PAD : 2 * PAD]) * r
        hid = (g / (1.0 + jnp.exp(-g)) * u).astype(BF)
        o = mm_nt(hid, wf[:, 2 * PAD : 3 * PAD])
        return [
            o[i * SLOTS : (i + 1) * SLOTS] + ob[pl.ds(pl.multiple_of(d * SLOTS, SLOTS), SLOTS), :]
            for i, d in enumerate(dests)
        ]

    chains = (
        (8, 1, 4, above, z_peer(5), szp, rzp, zp_s, zp_r, 0),
        (-7, -1, 3, below, z_peer(NZ - 5), szm, rzm, zm_s, zm_r, 0),
        (4, 1, 4, above, above, szp, rzp, zp_s, zp_r, 4),
        (-4, -1, 4, below, below, szm, rzm, zm_s, zm_r, 3),
    )
    z_copies = {}
    for t in range(4):
        live = [n for n in range(4) if t < chains[n][2]]
        dests = [(z + NZ + chains[n][0] - chains[n][1] * t) % NZ for n in live]
        if len(live) < 4:
            dests.append(z)
        vals = ffn(dests)
        for n, val in zip(live, vals):
            _, _, steps, target, last, out, got, ssem, rsem, base = chains[n]
            for h in (0, 1):
                part = val[h * CUT : (h + 1) * CUT]
                if t:
                    z_copies[n, t - 1, h].wait_recv()
                    part += got[base + t - 1, h].astype(F32)
                out[base + t, h] = part.astype(BF)
                c = remote(
                    out.at[base + t, h], got.at[base + t, h], ssem.at[base + t, h], rsem.at[base + t, h],
                    last if t == steps - 1 else target,
                )
                c.start()
                z_copies[n, t, h] = c
    mine = vals[-1]

    parts = []
    for h in (0, 1):
        val = mine[h * CUT : (h + 1) * CUT]
        for n in (1, 3, 2, 0):
            _, _, steps, _, _, _, got, _, _, base = chains[n]
            z_copies[n, steps - 1, h].wait_recv()
            val += got[base + steps - 1, h].astype(F32)
        parts.append(val)
    values = jnp.concatenate(parts, axis=0)
    vb = jnp.where(own, jnp.concatenate([values] * heads, axis=0), 0.0).astype(BF)
    out_ref[...] = mm(wt, vb)

    for c in raw_sends + rs_copies[0] + rs_copies[1] + w_copies + st_copies:
        c.wait_send()
    for i in range(SIDE):
        zi = jnp.where(k == 0, SIDE * y + i, SIDE * i + x)
        up_dist = (z - zi + NZ) % NZ
        down_dist = (zi - z + NZ) % NZ
        for part in range(4):

            @pl.when(jnp.logical_and(up_dist % 2 == 0, up_dist < UP_HOPS))
            def _():
                bc_send(i, part, True, 0).wait_send()
                bc_send(i, part, True, 1).wait_send()

            @pl.when(jnp.logical_and(down_dist % 2 == 0, down_dist < DOWN_HOPS))
            def _():
                bc_send(i, part, False, 0).wait_send()

            @pl.when(jnp.logical_and(down_dist % 2 == 0, down_dist + 2 <= DOWN_HOPS))
            def _():
                bc_send(i, part, False, 1).wait_send()

    for h in (0, 1):
        for t in range(UP_HOPS):
            p_send((z + NZ - t) % NZ, h, True).wait_send()
        for t in range(DOWN_HOPS):
            p_send((z + t) % NZ, h, False).wait_send()
    for c in z_copies.values():
        c.wait_send()


def body(enc_states, dec_states, segments, patch_keys, w_in, w_gate, w_up, w_down, w_out):
    nbytes, width = enc_states.shape
    depth, units = w_gate.shape
    local = w_in.shape[1]
    quarter = width // 8
    rows = NZ * SLOTS
    dma = pltpu.SemaphoreType.DMA
    vmem = pltpu.VMEM
    hbm = pl.BlockSpec(memory_space=pl.ANY)
    here = pl.BlockSpec(memory_space=pltpu.VMEM)
    mixed = pl.pallas_call(
        kernel,
        out_shape=jax.ShapeDtypeStruct((nbytes, width), F32),
        in_specs=[hbm, hbm, here, here, hbm, hbm, hbm, hbm, hbm],
        out_specs=here,
        scratch_shapes=[
            vmem((nbytes, width), BF),
            vmem((nbytes, width), BF),
            vmem((width, local), BF),
            vmem((local, width), BF),
            vmem((SIDE, 2, units, depth), BF),
            vmem((SIDE, 2, units, depth), BF),
            vmem((SIDE, 2, units, depth), BF),
            vmem((SIDE, 4, quarter // 2, local), BF),
            vmem((quarter, 2 * PAD), BF),
            vmem((quarter, PAD), BF),
            vmem((3, quarter, LANES[0]), BF),
            vmem((3, quarter, LANES[1]), BF),
            vmem((width, 3 * PAD), BF),
            vmem((NZ, SLOTS, width), BF),
            vmem((NZ, 1, rows), F32),
            vmem((NZ, SLOTS, HD), F32),
            vmem((rows, local), BF),
            vmem((rows, width), F32),
            vmem((UP_HOPS, 2, CUT, width), BF),
            vmem((UP_HOPS, 2, CUT, width), BF),
            vmem((DOWN_HOPS, 2, CUT, width), BF),
            vmem((DOWN_HOPS, 2, CUT, width), BF),
            vmem((SLOTS, width), F32),
            vmem((width // HD * SLOTS, nbytes), F32),
            dma((4,)), dma((7, 3)), dma((SIDE, 2, 3)), dma((3,)), dma((2,)),
            dma((SIDE, 4)), dma((SIDE, 4, 2)), dma((SIDE, 4, 2)),
            dma((2, 3)), dma((2, 3)), dma((62,)), dma((2, 2, SIDE, SIDE)),
            dma((NZ, 2)), dma((NZ, 2)), dma((NZ, 2)),
            dma((NZ,)), dma((NZ,)),
            dma((UP_HOPS, 2)), dma((UP_HOPS, 2)), dma((DOWN_HOPS, 2)), dma((DOWN_HOPS, 2)),
        ],
        compiler_params=pltpu.CompilerParams(
            collective_id=0, has_side_effects=True, vmem_limit_bytes=60 * 1024 * 1024
        ),
    )(
        enc_states, dec_states, segments.reshape(1, nbytes), patch_keys, w_in,
        w_gate.T, w_up.T, w_down, w_out,
    )
    return (dec_states.astype(F32) + mixed).astype(BF)


def solution(mesh):
    placed = (
        P(("seq", "mp"), None),
        P(("seq", "mp"), None),
        P(("seq", "mp")),
        P(("seq", "mp"), None),
        P(None, "mp"),
        P("seq", "mp"),
        P("seq", "mp"),
        P("mp", "seq"),
        P("mp", None),
    )
    return jax.shard_map(
        body, mesh=mesh, in_specs=placed, out_specs=P(("seq", "mp"), None), check_vma=False
    )
```

```python
import math

import jax
import jax.numpy as jnp
from jax import lax
from jax.experimental import pallas as pl
from jax.experimental.pallas import tpu as pltpu
from jax.sharding import PartitionSpec as P

MESH = pl.DeviceIdType.MESH
HD = 128
SIDE = 4
NZ = 16
SLOTS = 32
CUT = SLOTS // 2
BF = jnp.bfloat16
F32 = jnp.float32
EPS = 1e-05
NT = (((1,), (1,)), ((), ()))
UP_HOPS = 8
DOWN_HOPS = 7
PAD = 512
LANES = (2 * PAD // SIDE, PAD // SIDE)


def mm(a, b):
    return jnp.dot(a, b, preferred_element_type=F32)


def mm_nt(a, b):
    return lax.dot_general(a, b, NT, preferred_element_type=F32)


def kernel(
    enc_hbm, dec_hbm, seg_ref, keys_ref, win_hbm, wg_hbm, wu_hbm, wd_hbm, wout_hbm,
    out_ref,
    enc_ref, dec_ref, win_ref, wout_ref,
    rg, ru, rd, bc, ug, ud, rsg, rsd, wf, pall, st, rc, xs, ob, rzp, szp, rzm, szm, kpad, wts,
    in_s, raw_s, raw_r, loc_s, src_s, bc_r, bc_sp, bc_sm, rs_s, rs_r, w_s, w_r,
    p_r, p_sp, p_sm, st_r, st_s, zp_s, zp_r, zm_s, zm_r,
):
    s = lax.axis_index("seq")
    z = lax.axis_index("mp")
    k = s % 2
    x = (s // 2) % SIDE
    y = s // (2 * SIDE)
    a = x + k * (y - x)
    b = y + k * (x - y)
    width = enc_ref.shape[1]
    half = width // 2
    quarter = half // SIDE
    eighth = quarter // 2
    units = wg_hbm.shape[0]

    def dev(xx, yy, kk, zz):
        return {"seq": (yy * SIDE + xx) * 2 + kk, "mp": zz}

    def x_peer(j, kk):
        return dev((x + j) % SIDE, y, kk, z)

    def y_peer(j, kk):
        return dev(x, (y + j) % SIDE, kk, z)

    def a_peer(j):
        return dev((x + j * (1 - k)) % SIDE, (y + j * k) % SIDE, k, z)

    def b_peer(j):
        return dev((x + j * k) % SIDE, (y + j * (1 - k)) % SIDE, k, z)

    def z_peer(j):
        return dev(x, y, k, (z + j) % NZ)

    partner = dev(x, y, 1 - k, z)
    above = z_peer(1)
    below = z_peer(NZ - 1)

    barrier = pltpu.get_barrier_semaphore()
    above2 = z_peer(2)
    below2 = z_peer(NZ - 2)
    greeted = [above2, below2, above, below, partner]
    for j in (2, 1, 3):
        for kk in (0, 1):
            greeted += [x_peer(j, kk), y_peer(j, kk)]
    for d in greeted:
        pl.semaphore_signal(barrier, inc=1, device_id=d, device_id_type=MESH)

    def remote(src, dst, ssem, rsem, d):
        return pltpu.make_async_remote_copy(
            src_ref=src, dst_ref=dst, send_sem=ssem, recv_sem=rsem, device_id=d, device_id_type=MESH
        )

    loads = []
    for i, (src, dst) in enumerate(
        ((wout_hbm, wout_ref), (enc_hbm, enc_ref), (win_hbm, win_ref), (dec_hbm, dec_ref))
    ):
        c = pltpu.make_async_copy(src, dst, in_s.at[i])
        c.start()
        loads.append(c)

    def source(zz):
        hit0 = (zz // SIDE) == y
        hit1 = (zz % SIDE) == x
        hit = jnp.where(k == 0, hit0, hit1)
        slot = jnp.where(k == 0, zz % SIDE, zz // SIDE)
        return hit, slot

    first_row = k * half + a * quarter
    hit_me, slot_me = source(z)

    def src_copy(h):
        row = pl.multiple_of(first_row + h * eighth, 16)
        return pltpu.make_async_copy(win_hbm.at[pl.ds(row, eighth), :], bc.at[slot_me, h], src_s.at[h])

    @pl.when(hit_me)
    def _():
        src_copy(0).start()
        src_copy(1).start()

    raws = ((wg_hbm, rg), (wu_hbm, ru), (wd_hbm, rd))
    raw_local = []
    for i, (src, dst) in enumerate(raws):
        c = pltpu.make_async_copy(src, dst.at[a, k], loc_s.at[i])
        c.start()
        raw_local.append(c)

    pl.semaphore_wait(barrier, len(greeted))

    def bc_send(slot, part, up, far=0):
        sems = bc_sp if up else bc_sm
        target = ((below, below2), (above, above2))[up][far]
        view = bc.at[slot, part]
        return remote(view, view, sems.at[slot, part, far], bc_r.at[slot, part], target)

    def bc_spread(slot, part, up, far=True):
        if far:
            bc_send(slot, part, up, 1).start()
        bc_send(slot, part, up, 0).start()

    @pl.when(hit_me)
    def _():
        for h in (0, 1):
            src_copy(h).wait()
            bc_spread(slot_me, h, True)
            bc_spread(slot_me, h, False)

    raw_targets = [(partner, b)]
    for j in (1, 3, 2):
        raw_targets += [(x_peer(j, 0), x), (y_peer(j, 1), y)]
    raw_sends = []
    for i, (src, dst) in enumerate(raws):
        for n, (d, slot) in enumerate(raw_targets):
            c = remote(src, dst.at[slot, k], raw_s.at[n, i], raw_r.at[slot, k, i], d)
            c.start()
            raw_sends.append(c)

    def bc_turned():
        loads[0].wait()

        @pl.when(hit_me)
        def _():
            rows = lax.broadcasted_iota(jnp.int32, (quarter, width), 0) + first_row
            cols = lax.broadcasted_iota(jnp.int32, (quarter, width), 1)
            pick = jnp.where(rows == cols, 1.0, 0.0).astype(BF)
            turned = mm_nt(pick, wout_ref[...]).astype(BF)
            for h in (0, 1):
                bc[slot_me, 2 + h] = turned[h * eighth : (h + 1) * eighth]
                bc_spread(slot_me, 2 + h, True)
                bc_spread(slot_me, 2 + h, False)

    def bc_step(t, parts):
        if not 1 <= t <= UP_HOPS // 2:
            return
        for dist in (2 * t, 2 * t - 1):
            hit_u, slot_u = source((z + NZ - dist) % NZ)
            hit_d, slot_d = source((z + dist) % NZ)
            for part in parts:

                @pl.when(hit_u)
                def _():
                    bc_send(slot_u, part, True).wait_recv()
                    if dist % 2 == 0 and dist < UP_HOPS:
                        bc_spread(slot_u, part, True)

                if dist <= DOWN_HOPS:

                    @pl.when(hit_d)
                    def _():
                        bc_send(slot_d, part, False).wait_recv()
                        if dist % 2 == 0 and dist < DOWN_HOPS:
                            bc_spread(slot_d, part, False, dist + 2 <= DOWN_HOPS)

    loads[1].wait()
    member = lax.broadcasted_iota(jnp.int32, (SLOTS, enc_ref.shape[0]), 0) == seg_ref[...]
    member = jnp.where(member, 1.0, 0.0)
    lengths = jnp.maximum(jnp.sum(member, axis=1, keepdims=True), 1.0)
    pall[z] = (mm(member.astype(BF), enc_ref[...]) / lengths).astype(BF)

    def p_send(slot, h, up):
        view = pall.at[slot, pl.ds(h * CUT, CUT), :]
        ssem = p_sp if up else p_sm
        return remote(view, view, ssem.at[slot, h], p_r.at[slot, h], above if up else below)

    def p_step(t):
        if not 0 <= t <= UP_HOPS:
            return
        up_slot = (z + NZ - t) % NZ
        down_slot = (z + t) % NZ
        for h in (0, 1):
            if t:
                p_send(up_slot, h, True).wait_recv()
            if t < UP_HOPS:
                p_send(up_slot, h, True).start()
            if 1 <= t <= DOWN_HOPS:
                p_send(down_slot, h, False).wait_recv()
            if t < DOWN_HOPS:
                p_send(down_slot, h, False).start()

    ug[...] = jnp.zeros_like(ug)
    ud[...] = jnp.zeros_like(ud)
    p_step(0)
    bc_step(1, (0, 1))
    bc_turned()
    p_step(1)
    bc_step(2, (0, 1))
    p_step(2)
    bc_step(1, (2, 3))
    bc_step(3, (0, 1))
    p_step(3)
    bc_step(4, (0, 1))

    def raw_wait(i):
        raw_local[i].wait()
        src, dst = raws[i]
        for d in range(SIDE):
            for kk in (0, 1):

                @pl.when(jnp.logical_or(a != d, k != kk))
                def _():
                    remote(src, dst.at[d, kk], raw_s.at[0, 0], raw_r.at[d, kk, i], partner).wait_recv()

    def deep(buf):
        return jnp.concatenate([buf[i, kk] for i in range(SIDE) for kk in (0, 1)], axis=1)

    def tall(part):
        return jnp.concatenate(
            [jnp.concatenate([bc[i, part + h] for i in range(SIDE)], axis=1) for h in (0, 1)], axis=0
        )

    rs_copies = [[], []]

    def piece(part, bb, base=0):
        return pl.ds(pl.multiple_of(base + bb * LANES[part], 128), LANES[part])

    def rs_send(part):
        src, dst = ((ug, rsg), (ud, rsd))[part]
        for j in (2, 1, 3):
            c = remote(
                src.at[:, piece(part, (b + j) % SIDE)], dst.at[j - 1],
                rs_s.at[part, j - 1], rs_r.at[part, j - 1], b_peer(j),
            )
            c.start()
            rs_copies[part].append(c)

    def place(part, kk, aa, bb):
        row = pl.multiple_of(kk * half + aa * quarter, 32)
        return wf.at[pl.ds(row, quarter), piece(part, bb, part * 2 * PAD)]

    w_copies = []

    def w_send(part, kk, aa, bb, d):
        n = len(w_copies)
        view = place(part, kk, aa, bb)
        c = remote(view, view, w_s.at[n], w_r.at[part, kk, aa, bb], d)
        c.start()
        w_copies.append(c)

    def w_wait(part, kk, aa, bb):
        view = place(part, kk, aa, bb)
        remote(view, view, w_s.at[0], w_r.at[part, kk, aa, bb], partner).wait_recv()

    def w_sum(part):
        src, got = ((ug, rsg), (ud, rsd))[part]
        total = src[:, piece(part, b)].astype(F32)
        for c in rs_copies[part]:
            c.wait_recv()
        for j in (0, 1, 2):
            total += got[j].astype(F32)
        place(part, k, a, b)[...] = total.astype(BF)
        for j in (2, 1, 3):
            w_send(part, k, a, b, b_peer(j))
        for j in (2, 1, 3):
            w_send(part, k, a, b, a_peer(j))
        w_send(part, k, a, b, partner)

    def w_pass(part):
        for j in (1, 3, 2):
            bb = (b + j) % SIDE
            w_wait(part, k, a, bb)
            for i in (2, 1, 3):
                w_send(part, k, a, bb, a_peer(i))
            w_send(part, k, a, bb, partner)

    raw_wait(0)
    raw_wait(1)
    ins = tall(0)
    ug[:, 0:units] = mm_nt(ins, deep(rg)).astype(BF)
    ug[:, PAD : PAD + units] = mm_nt(ins, deep(ru)).astype(BF)
    rs_send(0)
    bc_step(2, (2, 3))
    p_step(4)
    bc_step(3, (2, 3))
    w_sum(0)
    p_step(5)
    bc_step(4, (2, 3))
    raw_wait(2)
    ud[:, 0:units] = mm_nt(tall(2), deep(rd)).astype(BF)
    rs_send(1)

    p_step(6)
    w_pass(0)
    w_sum(1)
    p_step(7)
    w_pass(1)
    p_step(8)

    loads[2].wait()
    rows = NZ * SLOTS
    for lo in range(0, NZ, 4):
        pr = pall[lo : lo + 4].reshape(4 * SLOTS, width)
        xr = mm(pr, win_ref[...]).astype(BF)
        xs[lo * SLOTS : (lo + 4) * SLOTS, :] = xr
        sq = xr.astype(F32)
        sq = sq * sq
        sq = sq[:, 0:128] + sq[:, 128:256]
        st[z, :, lo * SLOTS : (lo + 4) * SLOTS] = jnp.sum(jnp.transpose(sq), axis=0, keepdims=True)
    st_copies = []
    for j in (8, 7, 9, 6, 10, 5, 11, 4, 12, 3, 13, 2, 14, 1, 15):
        c = remote(st.at[z], st.at[z], st_s.at[j], st_r.at[z], z_peer(j))
        c.start()
        st_copies.append(c)
    for lo in range(0, rows, 4 * SLOTS):
        ob[lo : lo + 4 * SLOTS, :] = mm(xs[lo : lo + 4 * SLOTS, :], wout_ref[...])

    loads[3].wait()
    heads = width // HD
    kpad[...] = jnp.zeros_like(kpad)
    kpad[0 : keys_ref.shape[0], :] = keys_ref[...].astype(F32)
    own = lax.broadcasted_iota(jnp.int32, (heads * SLOTS, width), 0) // SLOTS
    own = own == lax.broadcasted_iota(jnp.int32, (heads * SLOTS, width), 1) // HD
    kb = jnp.where(own, jnp.concatenate([kpad[...]] * heads, axis=0), 0.0).astype(BF)
    scores = mm_nt(kb, dec_ref[...]) / math.sqrt(HD)
    allowed = lax.broadcasted_iota(jnp.int32, (SLOTS, dec_ref.shape[0]), 0) <= seg_ref[...]
    for h in range(heads):
        sc = jnp.where(allowed, scores[h * SLOTS : (h + 1) * SLOTS], -1e30)
        ex = jnp.exp(sc - jnp.max(sc, axis=0, keepdims=True))
        wts[h * SLOTS : (h + 1) * SLOTS, :] = ex / jnp.sum(ex, axis=0, keepdims=True)
    wt = jnp.transpose(wts[...]).astype(BF)

    for part in (0, 1):
        for j in (1, 3, 2):
            aa = (a + j) % SIDE
            for i in (0, 1, 3, 2):
                bb = (b + i) % SIDE
                w_wait(part, k, aa, bb)
                w_send(part, k, aa, bb, partner)

    for j in range(1, NZ):
        slot = (z + j) % NZ
        remote(st.at[slot], st.at[slot], st_s.at[0], st_r.at[slot], above).wait_recv()
    stat = st[0]
    for i in range(1, NZ):
        stat += st[i]
    inv = lax.rsqrt(stat / (NZ * win_ref.shape[1]) + EPS)
    for i in range(0, NZ, 4):
        r = jnp.transpose(jnp.broadcast_to(inv[:, i * SLOTS : (i + 4) * SLOTS], (HD, 4 * SLOTS)))
        rc[i : i + 4] = r.reshape(4, SLOTS, HD)

    for part in (0, 1):
        for aa in range(SIDE):
            for bb in range(SIDE):
                w_wait(part, 1 - k, aa, bb)

    def ffn(dests):
        pr = jnp.concatenate([pall[d] for d in dests], axis=0)
        r = jnp.concatenate([rc[d] for d in dests], axis=0)
        r = jnp.concatenate([r] * (PAD // HD), axis=1)
        g = mm(pr, wf[:, 0:PAD]) * r
        u = mm(pr, wf[:, PAD : 2 * PAD]) * r
        hid = (g / (1.0 + jnp.exp(-g)) * u).astype(BF)
        o = mm_nt(hid, wf[:, 2 * PAD : 3 * PAD])
        return [
            o[i * SLOTS : (i + 1) * SLOTS] + ob[pl.ds(pl.multiple_of(d * SLOTS, SLOTS), SLOTS), :]
            for i, d in enumerate(dests)
        ]

    chains = (
        (8, 1, 4, above, z_peer(5), szp, rzp, zp_s, zp_r, 0),
        (-7, -1, 3, below, z_peer(NZ - 5), szm, rzm, zm_s, zm_r, 0),
        (4, 1, 4, above, above, szp, rzp, zp_s, zp_r, 4),
        (-4, -1, 4, below, below, szm, rzm, zm_s, zm_r, 3),
    )
    z_copies = {}
    for t in range(4):
        live = [n for n in range(4) if t < chains[n][2]]
        dests = [(z + NZ + chains[n][0] - chains[n][1] * t) % NZ for n in live]
        if len(live) < 4:
            dests.append(z)
        vals = ffn(dests)
        for n, val in zip(live, vals):
            _, _, steps, target, last, out, got, ssem, rsem, base = chains[n]
            for h in (0, 1):
                part = val[h * CUT : (h + 1) * CUT]
                if t:
                    z_copies[n, t - 1, h].wait_recv()
                    part += got[base + t - 1, h].astype(F32)
                out[base + t, h] = part.astype(BF)
                c = remote(
                    out.at[base + t, h], got.at[base + t, h], ssem.at[base + t, h], rsem.at[base + t, h],
                    last if t == steps - 1 else target,
                )
                c.start()
                z_copies[n, t, h] = c
    mine = vals[-1]

    parts = []
    for h in (0, 1):
        val = mine[h * CUT : (h + 1) * CUT]
        for n in (1, 3, 2, 0):
            _, _, steps, _, _, _, got, _, _, base = chains[n]
            z_copies[n, steps - 1, h].wait_recv()
            val += got[base + steps - 1, h].astype(F32)
        parts.append(val)
    values = jnp.concatenate(parts, axis=0)
    vb = jnp.where(own, jnp.concatenate([values] * heads, axis=0), 0.0).astype(BF)
    out_ref[...] = mm(wt, vb)

    for c in raw_sends + rs_copies[0] + rs_copies[1] + w_copies + st_copies:
        c.wait_send()
    for i in range(SIDE):
        zi = jnp.where(k == 0, SIDE * y + i, SIDE * i + x)
        up_dist = (z - zi + NZ) % NZ
        down_dist = (zi - z + NZ) % NZ
        for part in range(4):

            @pl.when(jnp.logical_and(up_dist % 2 == 0, up_dist < UP_HOPS))
            def _():
                bc_send(i, part, True, 0).wait_send()
                bc_send(i, part, True, 1).wait_send()

            @pl.when(jnp.logical_and(down_dist % 2 == 0, down_dist < DOWN_HOPS))
            def _():
                bc_send(i, part, False, 0).wait_send()

            @pl.when(jnp.logical_and(down_dist % 2 == 0, down_dist + 2 <= DOWN_HOPS))
            def _():
                bc_send(i, part, False, 1).wait_send()

    for h in (0, 1):
        for t in range(UP_HOPS):
            p_send((z + NZ - t) % NZ, h, True).wait_send()
        for t in range(DOWN_HOPS):
            p_send((z + t) % NZ, h, False).wait_send()
    for c in z_copies.values():
        c.wait_send()


def body(enc_states, dec_states, segments, patch_keys, w_in, w_gate, w_up, w_down, w_out):
    nbytes, width = enc_states.shape
    depth, units = w_gate.shape
    local = w_in.shape[1]
    quarter = width // 8
    rows = NZ * SLOTS
    dma = pltpu.SemaphoreType.DMA
    vmem = pltpu.VMEM
    hbm = pl.BlockSpec(memory_space=pl.ANY)
    here = pl.BlockSpec(memory_space=pltpu.VMEM)
    mixed = pl.pallas_call(
        kernel,
        out_shape=jax.ShapeDtypeStruct((nbytes, width), F32),
        in_specs=[hbm, hbm, here, here, hbm, hbm, hbm, hbm, hbm],
        out_specs=here,
        scratch_shapes=[
            vmem((nbytes, width), BF),
            vmem((nbytes, width), BF),
            vmem((width, local), BF),
            vmem((local, width), BF),
            vmem((SIDE, 2, units, depth), BF),
            vmem((SIDE, 2, units, depth), BF),
            vmem((SIDE, 2, units, depth), BF),
            vmem((SIDE, 4, quarter // 2, local), BF),
            vmem((quarter, 2 * PAD), BF),
            vmem((quarter, PAD), BF),
            vmem((3, quarter, LANES[0]), BF),
            vmem((3, quarter, LANES[1]), BF),
            vmem((width, 3 * PAD), BF),
            vmem((NZ, SLOTS, width), BF),
            vmem((NZ, 1, rows), F32),
            vmem((NZ, SLOTS, HD), F32),
            vmem((rows, local), BF),
            vmem((rows, width), F32),
            vmem((UP_HOPS, 2, CUT, width), BF),
            vmem((UP_HOPS, 2, CUT, width), BF),
            vmem((DOWN_HOPS, 2, CUT, width), BF),
            vmem((DOWN_HOPS, 2, CUT, width), BF),
            vmem((SLOTS, width), F32),
            vmem((width // HD * SLOTS, nbytes), F32),
            dma((4,)), dma((7, 3)), dma((SIDE, 2, 3)), dma((3,)), dma((2,)),
            dma((SIDE, 4)), dma((SIDE, 4, 2)), dma((SIDE, 4, 2)),
            dma((2, 3)), dma((2, 3)), dma((62,)), dma((2, 2, SIDE, SIDE)),
            dma((NZ, 2)), dma((NZ, 2)), dma((NZ, 2)),
            dma((NZ,)), dma((NZ,)),
            dma((UP_HOPS, 2)), dma((UP_HOPS, 2)), dma((DOWN_HOPS, 2)), dma((DOWN_HOPS, 2)),
        ],
        compiler_params=pltpu.CompilerParams(
            collective_id=0, has_side_effects=True, vmem_limit_bytes=60 * 1024 * 1024
        ),
    )(
        enc_states, dec_states, segments.reshape(1, nbytes), patch_keys, w_in,
        w_gate.T, w_up.T, w_down, w_out,
    )
    return (dec_states.astype(F32) + mixed).astype(BF)


def solution(mesh):
    placed = (
        P(("seq", "mp"), None),
        P(("seq", "mp"), None),
        P(("seq", "mp")),
        P(("seq", "mp"), None),
        P(None, "mp"),
        P("seq", "mp"),
        P("seq", "mp"),
        P("mp", "seq"),
        P("mp", None),
    )
    return jax.shard_map(
        body, mesh=mesh, in_specs=placed, out_specs=P(("seq", "mp"), None), check_vma=False
    )
```

```python
import math

import jax
import jax.numpy as jnp
from jax import lax
from jax.experimental import pallas as pl
from jax.experimental.pallas import tpu as pltpu
from jax.sharding import PartitionSpec as P

MESH = pl.DeviceIdType.MESH
HD = 128
SIDE = 4
NZ = 16
SLOTS = 32
CUT = SLOTS // 2
BF = jnp.bfloat16
F32 = jnp.float32
EPS = 1e-05
NT = (((1,), (1,)), ((), ()))
UP_HOPS = 8
DOWN_HOPS = 7
PAD = 512
LANES = (2 * PAD // SIDE, PAD // SIDE)


def mm(a, b):
    return jnp.dot(a, b, preferred_element_type=F32)


def mm_nt(a, b):
    return lax.dot_general(a, b, NT, preferred_element_type=F32)


def kernel(
    enc_hbm, dec_hbm, seg_ref, keys_ref, win_hbm, wg_hbm, wu_hbm, wd_hbm, wout_hbm,
    out_ref,
    enc_ref, dec_ref, win_ref, wout_ref,
    rg, ru, rd, bc, ug, ud, rsg, rsd, wf, pall, st, rc, xs, ob, rzp, szp, rzm, szm, kpad, wts,
    in_s, raw_s, raw_r, loc_s, src_s, bc_r, bc_sp, bc_sm, rs_s, rs_r, w_s, w_r,
    p_r, p_sp, p_sm, st_r, st_s, zp_s, zp_r, zm_s, zm_r,
):
    s = lax.axis_index("seq")
    z = lax.axis_index("mp")
    k = s % 2
    x = (s // 2) % SIDE
    y = s // (2 * SIDE)
    a = x + k * (y - x)
    b = y + k * (x - y)
    width = enc_ref.shape[1]
    half = width // 2
    quarter = half // SIDE
    eighth = quarter // 2
    units = wg_hbm.shape[0]

    def dev(xx, yy, kk, zz):
        return {"seq": (yy * SIDE + xx) * 2 + kk, "mp": zz}

    def x_peer(j, kk):
        return dev((x + j) % SIDE, y, kk, z)

    def y_peer(j, kk):
        return dev(x, (y + j) % SIDE, kk, z)

    def a_peer(j):
        return dev((x + j * (1 - k)) % SIDE, (y + j * k) % SIDE, k, z)

    def b_peer(j):
        return dev((x + j * k) % SIDE, (y + j * (1 - k)) % SIDE, k, z)

    def z_peer(j):
        return dev(x, y, k, (z + j) % NZ)

    partner = dev(x, y, 1 - k, z)
    above = z_peer(1)
    below = z_peer(NZ - 1)

    barrier = pltpu.get_barrier_semaphore()
    above2 = z_peer(2)
    below2 = z_peer(NZ - 2)
    greeted = [above2, below2, above, below, partner]
    for j in (2, 1, 3):
        for kk in (0, 1):
            greeted += [x_peer(j, kk), y_peer(j, kk)]
    for d in greeted:
        pl.semaphore_signal(barrier, inc=1, device_id=d, device_id_type=MESH)

    def remote(src, dst, ssem, rsem, d):
        return pltpu.make_async_remote_copy(
            src_ref=src, dst_ref=dst, send_sem=ssem, recv_sem=rsem, device_id=d, device_id_type=MESH
        )

    loads = []
    for i, (src, dst) in enumerate(
        ((wout_hbm, wout_ref), (enc_hbm, enc_ref), (win_hbm, win_ref), (dec_hbm, dec_ref))
    ):
        c = pltpu.make_async_copy(src, dst, in_s.at[i])
        c.start()
        loads.append(c)

    def source(zz):
        hit0 = (zz // SIDE) == y
        hit1 = (zz % SIDE) == x
        hit = jnp.where(k == 0, hit0, hit1)
        slot = jnp.where(k == 0, zz % SIDE, zz // SIDE)
        return hit, slot

    first_row = k * half + a * quarter
    hit_me, slot_me = source(z)

    def src_copy(h):
        row = pl.multiple_of(first_row + h * eighth, 16)
        return pltpu.make_async_copy(win_hbm.at[pl.ds(row, eighth), :], bc.at[slot_me, h], src_s.at[h])

    @pl.when(hit_me)
    def _():
        src_copy(0).start()
        src_copy(1).start()

    raws = ((wg_hbm, rg), (wu_hbm, ru), (wd_hbm, rd))
    raw_local = []
    for i, (src, dst) in enumerate(raws):
        c = pltpu.make_async_copy(src, dst.at[a, k], loc_s.at[i])
        c.start()
        raw_local.append(c)

    pl.semaphore_wait(barrier, len(greeted))

    def bc_send(slot, part, up, far=0):
        sems = bc_sp if up else bc_sm
        target = ((below, below2), (above, above2))[up][far]
        view = bc.at[slot, part]
        return remote(view, view, sems.at[slot, part, far], bc_r.at[slot, part], target)

    def bc_spread(slot, part, up, far=True):
        if far:
            bc_send(slot, part, up, 1).start()
        bc_send(slot, part, up, 0).start()

    @pl.when(hit_me)
    def _():
        for h in (0, 1):
            src_copy(h).wait()
            bc_spread(slot_me, h, True)
            bc_spread(slot_me, h, False)

    raw_targets = [(partner, b)]
    for j in (1, 3, 2):
        raw_targets += [(x_peer(j, 0), x), (y_peer(j, 1), y)]
    raw_sends = []
    for i, (src, dst) in enumerate(raws):
        for n, (d, slot) in enumerate(raw_targets):
            c = remote(src, dst.at[slot, k], raw_s.at[n, i], raw_r.at[slot, k, i], d)
            c.start()
            raw_sends.append(c)

    def bc_turned():
        loads[0].wait()

        @pl.when(hit_me)
        def _():
            rows = lax.broadcasted_iota(jnp.int32, (quarter, width), 0) + first_row
            cols = lax.broadcasted_iota(jnp.int32, (quarter, width), 1)
            pick = jnp.where(rows == cols, 1.0, 0.0).astype(BF)
            turned = mm_nt(pick, wout_ref[...]).astype(BF)
            for h in (0, 1):
                bc[slot_me, 2 + h] = turned[h * eighth : (h + 1) * eighth]
                bc_spread(slot_me, 2 + h, True)
                bc_spread(slot_me, 2 + h, False)

    def bc_step(t, parts):
        if not 1 <= t <= UP_HOPS // 2:
            return
        for dist in (2 * t, 2 * t - 1):
            hit_u, slot_u = source((z + NZ - dist) % NZ)
            hit_d, slot_d = source((z + dist) % NZ)
            for part in parts:

                @pl.when(hit_u)
                def _():
                    bc_send(slot_u, part, True).wait_recv()
                    if dist % 2 == 0 and dist < UP_HOPS:
                        bc_spread(slot_u, part, True)

                if dist <= DOWN_HOPS:

                    @pl.when(hit_d)
                    def _():
                        bc_send(slot_d, part, False).wait_recv()
                        if dist % 2 == 0 and dist < DOWN_HOPS:
                            bc_spread(slot_d, part, False, dist + 2 <= DOWN_HOPS)

    loads[1].wait()
    member = lax.broadcasted_iota(jnp.int32, (SLOTS, enc_ref.shape[0]), 0) == seg_ref[...]
    member = jnp.where(member, 1.0, 0.0)
    lengths = jnp.maximum(jnp.sum(member, axis=1, keepdims=True), 1.0)
    pall[z] = (mm(member.astype(BF), enc_ref[...]) / lengths).astype(BF)

    def p_send(slot, h, up):
        view = pall.at[slot, pl.ds(h * CUT, CUT), :]
        ssem = p_sp if up else p_sm
        return remote(view, view, ssem.at[slot, h], p_r.at[slot, h], above if up else below)

    def p_step(t):
        if not 0 <= t <= UP_HOPS:
            return
        up_slot = (z + NZ - t) % NZ
        down_slot = (z + t) % NZ
        for h in (0, 1):
            if t:
                p_send(up_slot, h, True).wait_recv()
            if t < UP_HOPS:
                p_send(up_slot, h, True).start()
            if 1 <= t <= DOWN_HOPS:
                p_send(down_slot, h, False).wait_recv()
            if t < DOWN_HOPS:
                p_send(down_slot, h, False).start()

    ug[...] = jnp.zeros_like(ug)
    ud[...] = jnp.zeros_like(ud)
    p_step(0)
    bc_step(1, (0, 1))
    bc_turned()
    p_step(1)
    bc_step(2, (0, 1))
    p_step(2)
    bc_step(1, (2, 3))
    bc_step(3, (0, 1))
    bc_step(4, (0, 1))

    def raw_wait(i):
        raw_local[i].wait()
        src, dst = raws[i]
        for d in range(SIDE):
            for kk in (0, 1):

                @pl.when(jnp.logical_or(a != d, k != kk))
                def _():
                    remote(src, dst.at[d, kk], raw_s.at[0, 0], raw_r.at[d, kk, i], partner).wait_recv()

    def deep(buf):
        return jnp.concatenate([buf[i, kk] for i in range(SIDE) for kk in (0, 1)], axis=1)

    def tall(part):
        return jnp.concatenate(
            [jnp.concatenate([bc[i, part + h] for i in range(SIDE)], axis=1) for h in (0, 1)], axis=0
        )

    rs_copies = [[], []]

    def piece(part, bb, base=0):
        return pl.ds(pl.multiple_of(base + bb * LANES[part], 128), LANES[part])

    def rs_send(part):
        src, dst = ((ug, rsg), (ud, rsd))[part]
        for j in (2, 1, 3):
            c = remote(
                src.at[:, piece(part, (b + j) % SIDE)], dst.at[j - 1],
                rs_s.at[part, j - 1], rs_r.at[part, j - 1], b_peer(j),
            )
            c.start()
            rs_copies[part].append(c)

    def place(part, kk, aa, bb):
        row = pl.multiple_of(kk * half + aa * quarter, 32)
        return wf.at[pl.ds(row, quarter), piece(part, bb, part * 2 * PAD)]

    w_copies = []

    def w_send(part, kk, aa, bb, d):
        n = len(w_copies)
        view = place(part, kk, aa, bb)
        c = remote(view, view, w_s.at[n], w_r.at[part, kk, aa, bb], d)
        c.start()
        w_copies.append(c)

    def w_wait(part, kk, aa, bb):
        view = place(part, kk, aa, bb)
        remote(view, view, w_s.at[0], w_r.at[part, kk, aa, bb], partner).wait_recv()

    def w_sum(part):
        src, got = ((ug, rsg), (ud, rsd))[part]
        total = src[:, piece(part, b)].astype(F32)
        for c in rs_copies[part]:
            c.wait_recv()
        for j in (0, 1, 2):
            total += got[j].astype(F32)
        place(part, k, a, b)[...] = total.astype(BF)
        for j in (2, 1, 3):
            w_send(part, k, a, b, b_peer(j))
        for j in (2, 1, 3):
            w_send(part, k, a, b, a_peer(j))
        w_send(part, k, a, b, partner)

    def w_pass(part):
        for j in (1, 3, 2):
            bb = (b + j) % SIDE
            w_wait(part, k, a, bb)
            for i in (2, 1, 3):
                w_send(part, k, a, bb, a_peer(i))
            w_send(part, k, a, bb, partner)

    raw_wait(0)
    raw_wait(1)
    ins = tall(0)
    ug[:, 0:units] = mm_nt(ins, deep(rg)).astype(BF)
    ug[:, PAD : PAD + units] = mm_nt(ins, deep(ru)).astype(BF)
    rs_send(0)
    bc_step(2, (2, 3))
    p_step(3)
    w_sum(0)
    bc_step(3, (2, 3))
    p_step(4)
    w_pass(0)
    bc_step(4, (2, 3))
    raw_wait(2)
    ud[:, 0:units] = mm_nt(tall(2), deep(rd)).astype(BF)
    rs_send(1)

    p_step(5)
    p_step(6)
    w_sum(1)
    p_step(7)
    w_pass(1)
    p_step(8)

    loads[2].wait()
    rows = NZ * SLOTS
    for lo in range(0, NZ, 4):
        pr = pall[lo : lo + 4].reshape(4 * SLOTS, width)
        xr = mm(pr, win_ref[...]).astype(BF)
        xs[lo * SLOTS : (lo + 4) * SLOTS, :] = xr
        sq = xr.astype(F32)
        sq = sq * sq
        sq = sq[:, 0:128] + sq[:, 128:256]
        st[z, :, lo * SLOTS : (lo + 4) * SLOTS] = jnp.sum(jnp.transpose(sq), axis=0, keepdims=True)
    st_copies = []
    for j in (8, 7, 9, 6, 10, 5, 11, 4, 12, 3, 13, 2, 14, 1, 15):
        c = remote(st.at[z], st.at[z], st_s.at[j], st_r.at[z], z_peer(j))
        c.start()
        st_copies.append(c)
    for lo in range(0, rows, 4 * SLOTS):
        ob[lo : lo + 4 * SLOTS, :] = mm(xs[lo : lo + 4 * SLOTS, :], wout_ref[...])

    loads[3].wait()
    heads = width // HD
    kpad[...] = jnp.zeros_like(kpad)
    kpad[0 : keys_ref.shape[0], :] = keys_ref[...].astype(F32)
    own = lax.broadcasted_iota(jnp.int32, (heads * SLOTS, width), 0) // SLOTS
    own = own == lax.broadcasted_iota(jnp.int32, (heads * SLOTS, width), 1) // HD
    kb = jnp.where(own, jnp.concatenate([kpad[...]] * heads, axis=0), 0.0).astype(BF)
    scores = mm_nt(kb, dec_ref[...]) / math.sqrt(HD)
    allowed = lax.broadcasted_iota(jnp.int32, (SLOTS, dec_ref.shape[0]), 0) <= seg_ref[...]
    for h in range(heads):
        sc = jnp.where(allowed, scores[h * SLOTS : (h + 1) * SLOTS], -1e30)
        ex = jnp.exp(sc - jnp.max(sc, axis=0, keepdims=True))
        wts[h * SLOTS : (h + 1) * SLOTS, :] = ex / jnp.sum(ex, axis=0, keepdims=True)
    wt = jnp.transpose(wts[...]).astype(BF)

    for part in (0, 1):
        for j in (1, 3, 2):
            aa = (a + j) % SIDE
            for i in (0, 1, 3, 2):
                bb = (b + i) % SIDE
                w_wait(part, k, aa, bb)
                w_send(part, k, aa, bb, partner)

    for j in range(1, NZ):
        slot = (z + j) % NZ
        remote(st.at[slot], st.at[slot], st_s.at[0], st_r.at[slot], above).wait_recv()
    stat = st[0]
    for i in range(1, NZ):
        stat += st[i]
    inv = lax.rsqrt(stat / (NZ * win_ref.shape[1]) + EPS)
    for i in range(0, NZ, 4):
        r = jnp.transpose(jnp.broadcast_to(inv[:, i * SLOTS : (i + 4) * SLOTS], (HD, 4 * SLOTS)))
        rc[i : i + 4] = r.reshape(4, SLOTS, HD)

    for part in (0, 1):
        for aa in range(SIDE):
            for bb in range(SIDE):
                w_wait(part, 1 - k, aa, bb)

    def ffn(dests):
        pr = jnp.concatenate([pall[d] for d in dests], axis=0)
        r = jnp.concatenate([rc[d] for d in dests], axis=0)
        r = jnp.concatenate([r] * (PAD // HD), axis=1)
        g = mm(pr, wf[:, 0:PAD]) * r
        u = mm(pr, wf[:, PAD : 2 * PAD]) * r
        hid = (g / (1.0 + jnp.exp(-g)) * u).astype(BF)
        o = mm_nt(hid, wf[:, 2 * PAD : 3 * PAD])
        return [
            o[i * SLOTS : (i + 1) * SLOTS] + ob[pl.ds(pl.multiple_of(d * SLOTS, SLOTS), SLOTS), :]
            for i, d in enumerate(dests)
        ]

    chains = (
        (8, 1, 4, above, z_peer(5), szp, rzp, zp_s, zp_r, 0),
        (-7, -1, 3, below, z_peer(NZ - 5), szm, rzm, zm_s, zm_r, 0),
        (4, 1, 4, above, above, szp, rzp, zp_s, zp_r, 4),
        (-4, -1, 4, below, below, szm, rzm, zm_s, zm_r, 3),
    )
    z_copies = {}
    for t in range(4):
        live = [n for n in range(4) if t < chains[n][2]]
        dests = [(z + NZ + chains[n][0] - chains[n][1] * t) % NZ for n in live]
        if len(live) < 4:
            dests.append(z)
        vals = ffn(dests)
        for n, val in zip(live, vals):
            _, _, steps, target, last, out, got, ssem, rsem, base = chains[n]
            for h in (0, 1):
                part = val[h * CUT : (h + 1) * CUT]
                if t:
                    z_copies[n, t - 1, h].wait_recv()
                    part += got[base + t - 1, h].astype(F32)
                out[base + t, h] = part.astype(BF)
                c = remote(
                    out.at[base + t, h], got.at[base + t, h], ssem.at[base + t, h], rsem.at[base + t, h],
                    last if t == steps - 1 else target,
                )
                c.start()
                z_copies[n, t, h] = c
    mine = vals[-1]

    parts = []
    for h in (0, 1):
        val = mine[h * CUT : (h + 1) * CUT]
        for n in (1, 3, 2, 0):
            _, _, steps, _, _, _, got, _, _, base = chains[n]
            z_copies[n, steps - 1, h].wait_recv()
            val += got[base + steps - 1, h].astype(F32)
        parts.append(val)
    values = jnp.concatenate(parts, axis=0)
    vb = jnp.where(own, jnp.concatenate([values] * heads, axis=0), 0.0).astype(BF)
    out_ref[...] = mm(wt, vb).astype(BF)

    for c in raw_sends + rs_copies[0] + rs_copies[1] + w_copies + st_copies:
        c.wait_send()
    for i in range(SIDE):
        zi = jnp.where(k == 0, SIDE * y + i, SIDE * i + x)
        up_dist = (z - zi + NZ) % NZ
        down_dist = (zi - z + NZ) % NZ
        for part in range(4):

            @pl.when(jnp.logical_and(up_dist % 2 == 0, up_dist < UP_HOPS))
            def _():
                bc_send(i, part, True, 0).wait_send()
                bc_send(i, part, True, 1).wait_send()

            @pl.when(jnp.logical_and(down_dist % 2 == 0, down_dist < DOWN_HOPS))
            def _():
                bc_send(i, part, False, 0).wait_send()

            @pl.when(jnp.logical_and(down_dist % 2 == 0, down_dist + 2 <= DOWN_HOPS))
            def _():
                bc_send(i, part, False, 1).wait_send()

    for h in (0, 1):
        for t in range(UP_HOPS):
            p_send((z + NZ - t) % NZ, h, True).wait_send()
        for t in range(DOWN_HOPS):
            p_send((z + t) % NZ, h, False).wait_send()
    for c in z_copies.values():
        c.wait_send()


def body(enc_states, dec_states, segments, patch_keys, w_in, w_gate, w_up, w_down, w_out):
    nbytes, width = enc_states.shape
    depth, units = w_gate.shape
    local = w_in.shape[1]
    quarter = width // 8
    rows = NZ * SLOTS
    dma = pltpu.SemaphoreType.DMA
    vmem = pltpu.VMEM
    hbm = pl.BlockSpec(memory_space=pl.ANY)
    here = pl.BlockSpec(memory_space=pltpu.VMEM)
    mixed = pl.pallas_call(
        kernel,
        out_shape=jax.ShapeDtypeStruct((nbytes, width), BF),
        in_specs=[hbm, hbm, here, here, hbm, hbm, hbm, hbm, hbm],
        out_specs=here,
        scratch_shapes=[
            vmem((nbytes, width), BF),
            vmem((nbytes, width), BF),
            vmem((width, local), BF),
            vmem((local, width), BF),
            vmem((SIDE, 2, units, depth), BF),
            vmem((SIDE, 2, units, depth), BF),
            vmem((SIDE, 2, units, depth), BF),
            vmem((SIDE, 4, quarter // 2, local), BF),
            vmem((quarter, 2 * PAD), BF),
            vmem((quarter, PAD), BF),
            vmem((3, quarter, LANES[0]), BF),
            vmem((3, quarter, LANES[1]), BF),
            vmem((width, 3 * PAD), BF),
            vmem((NZ, SLOTS, width), BF),
            vmem((NZ, 1, rows), F32),
            vmem((NZ, SLOTS, HD), F32),
            vmem((rows, local), BF),
            vmem((rows, width), F32),
            vmem((UP_HOPS, 2, CUT, width), BF),
            vmem((UP_HOPS, 2, CUT, width), BF),
            vmem((DOWN_HOPS, 2, CUT, width), BF),
            vmem((DOWN_HOPS, 2, CUT, width), BF),
            vmem((SLOTS, width), F32),
            vmem((width // HD * SLOTS, nbytes), F32),
            dma((4,)), dma((7, 3)), dma((SIDE, 2, 3)), dma((3,)), dma((2,)),
            dma((SIDE, 4)), dma((SIDE, 4, 2)), dma((SIDE, 4, 2)),
            dma((2, 3)), dma((2, 3)), dma((62,)), dma((2, 2, SIDE, SIDE)),
            dma((NZ, 2)), dma((NZ, 2)), dma((NZ, 2)),
            dma((NZ,)), dma((NZ,)),
            dma((UP_HOPS, 2)), dma((UP_HOPS, 2)), dma((DOWN_HOPS, 2)), dma((DOWN_HOPS, 2)),
        ],
        compiler_params=pltpu.CompilerParams(
            collective_id=0, has_side_effects=True, vmem_limit_bytes=60 * 1024 * 1024
        ),
    )(
        enc_states, dec_states, segments.reshape(1, nbytes), patch_keys, w_in,
        w_gate.T, w_up.T, w_down, w_out,
    )
    return (dec_states.astype(F32) + mixed.astype(F32)).astype(BF)


def solution(mesh):
    placed = (
        P(("seq", "mp"), None),
        P(("seq", "mp"), None),
        P(("seq", "mp")),
        P(("seq", "mp"), None),
        P(None, "mp"),
        P("seq", "mp"),
        P("seq", "mp"),
        P("mp", "seq"),
        P("mp", None),
    )
    return jax.shard_map(
        body, mesh=mesh, in_specs=placed, out_specs=P(("seq", "mp"), None), check_vma=False
    )
```
